32 devices in a mesh: rep: 2 (over x), shard: 16 (over z, y, core).
Axes of the slice: x: 2, y: 2, z: 4, core: 2. Of those that a mesh axis runs over, the one named last changes fastest.
Arguments:
- tokens: bfloat16 [32, 192, 2048], P(('rep', 'shard')), may hold values from -7 to 7
- segment_ids: int32 [32, 192], P(('rep', 'shard')), may hold values from 0 to 3, never falling along the last dimension, each value on 1 to 96 neighbouring positions
- norm_gain: bfloat16 [2048], P('shard'), may hold values from 0.25 to 1.75
- input_weight: bfloat16 [2048, 2048], P('shard'), may hold values from -0.125 to 0.125
- forget_weight: bfloat16 [2048, 2048], P('shard'), may hold values from -0.5 to 0.5
- gate_weight: bfloat16 [2048, 2048], P('shard'), may hold values from -0.125 to 0.125
- mixer_gain: bfloat16 [2048], P('shard'), may hold values from 0.25 to 1.75
- out_weight: bfloat16 [2048, 2048], P('shard'), may hold values from -0.1875 to 0.1875
- ffn_gain: bfloat16 [2048], P('shard'), may hold values from 0.25 to 1.75
- ffn_gate_weight: bfloat16 [2048, 5632], P('shard'), may hold values from -0.125 to 0.125
- ffn_up_weight: bfloat16 [2048, 5632], P('shard'), may hold values from -0.125 to 0.125
- ffn_down_weight: bfloat16 [5632, 2048], P('shard'), may hold values from -0.15625 to 0.15625
- cotangent: bfloat16 [32, 192, 2048], P(('rep', 'shard')), may hold values from -6 to 6
Outputs:
- block_output: bfloat16 [32, 192, 2048], P(('rep', 'shard'))
- input_grad: bfloat16 [32, 192, 2048], P(('rep', 'shard'))
- norm_gain_grad: float32 [2048], P('shard')
- input_weight_grad: float32 [2048, 2048], P('shard')
- forget_weight_grad: float32 [2048, 2048], P('shard')
- gate_weight_grad: float32 [2048, 2048], P('shard')
- mixer_gain_grad: float32 [2048], P('shard')
- out_weight_grad: float32 [2048, 2048], P('shard')
- ffn_gain_grad: float32 [2048], P('shard')
- ffn_gate_grad: float32 [2048, 5632], P('shard')
- ffn_up_grad: float32 [2048, 5632], P('shard')
- ffn_down_grad: float32 [5632, 2048], P('shard')
The draws below stay inside these ranges and needn't reach their ends.
Inputs may be any that keep to these rules, and one draw needn't show every extreme that they name: `segment_ids`: document numbers never fall along a sequence; each document has 1 to 96 tokens, and one has exactly 96.
All inputs are finite; a program needn't handle non-finite values.
Results may differ from the reference program's by a relative error of at most 0.019.
Values may be sent and summed in bfloat16 or wider, within the bound.
No kernel may reach another device: no remote copies, remote signals or barrier semaphores. Data moves between devices by JAX's collectives and lax.ppermute only.
A program may use at most 640 MiB of HBM per device.

```python
import math
import jax
import jax.numpy as jnp
import numpy as np
from jax import lax

D = 2048
FF = 5632
LEN = 192
SEQS = 32


def common_direction(key):
    return jnp.clip(jax.random.normal(jax.random.fold_in(key, 7), (D,), jnp.float32), -3.0, 3.0)


def draw_tokens(key, part):
    direction = common_direction(key)
    noise_key = jax.random.fold_in(key, 11)
    noise = jnp.clip(jax.random.normal(noise_key, (SEQS, LEN, D), jnp.float32), -4.0, 4.0)
    return (direction[None, None, :] + noise).astype(jnp.bfloat16)


def draw_forget_weight(key, part):
    direction = common_direction(key)
    noise = jnp.clip(jax.random.normal(jax.random.fold_in(key, 13), (D, D), jnp.float32), -6.0, 6.0)
    noise = noise * (1.0 / D ** 0.5)
    picked = jax.random.uniform(jax.random.fold_in(key, 17), (D,), jnp.float32)
    levels = jax.random.uniform(jax.random.fold_in(key, 19), (D,), jnp.float32, 3.5, 6.5)
    share = 0.6
    target = jnp.where(picked < share, levels, 0.0)
    aligned = direction[:, None] * (target * 2.0 ** 0.5 / D)[None, :]
    return (noise + aligned).astype(jnp.bfloat16)


def shard_levels(key, dims, pieces, smallest, high):
    factor_of, own = 1.0, jax.random.fold_in(key, 6)
    for position, shards_of in pieces:
        heights = jnp.exp(jax.random.uniform(jax.random.fold_in(own, position), (shards_of,), jnp.float32, smallest / len(pieces), high / len(pieces)))
        factor_of = factor_of * jnp.repeat(heights, dims[position] // shards_of).reshape([-1 if axis == position else 1 for axis in range(len(dims))])
    return factor_of


def split_up(count, total, most, skew):
    loads = [(1 << 20) // math.isqrt(standing ** skew) + 1 for standing in range(2, count + 1)]
    rest, counts = total - most - (count - 1), [1] * (count - 1)
    while rest > 0:
        movable = [i for i in range(count - 1) if counts[i] < most]
        pool, budget = sum([loads[i] for i in movable]), rest
        for i in movable:
            addition = min(most - counts[i], max(1, budget * loads[i] // pool), rest)
            counts[i] = counts[i] + addition
            rest = rest - addition
    return np.array([most] + counts)


def uneven(own_key, count, total, limit, slope):
    if count == 2:
        one = jax.random.randint(own_key, (), max(1, total - limit), min(limit, total - 1) + 1)
        return jnp.stack([one, total - one])
    sizes = jnp.asarray(split_up(count, total, limit, slope), jnp.int32)
    pairs = (count - 1) // 2
    donor, taker = sizes[1:1 + 2 * pairs:2], sizes[2:2 + 2 * pairs:2]
    room = jnp.minimum(donor - 1, limit - taker)
    passed = jax.random.randint(jax.random.fold_in(own_key, 1), (pairs,), 0, 1 << 20) % (room + 1)
    sizes = sizes.at[1:1 + 2 * pairs:2].set(donor - passed).at[2:2 + 2 * pairs:2].set(taker + passed)
    return sizes[jax.random.permutation(jax.random.fold_in(own_key, 2), count)]


def scatter_about(key, extent, scale, most, shards=(), held_as=jnp.bfloat16):
    array = jax.random.normal(key, extent, jnp.float32) * scale
    if len(shards) > 0:
        array = shard_levels(key, extent, shards, -0.22, 0.18) * array
    return jnp.clip(array, min=-most, max=most).astype(held_as)


def setup_inputs(seed: int = 0) -> dict:
    keys = jax.random.split(jax.random.key(seed), 14)
    tokens = draw_tokens(jax.random.fold_in(keys[13], 71), 0)
    segment_ids = jax.vmap(lambda own: jnp.searchsorted(jnp.cumsum(uneven(own, max(4, LEN // 48), LEN, LEN // 2, 2)), jnp.arange(LEN), side="right"))(jax.random.split(keys[1], SEQS)).reshape((SEQS, LEN)).astype(jnp.int32)
    norm_gain = jnp.clip(1.0 + 0.15 * jax.random.normal(keys[2], (D,), jnp.float32), 0.25, 1.75).astype(jnp.bfloat16)
    input_weight = scatter_about(keys[3], (D, D), D ** -0.5, 0.125, ((0, 16),))
    forget_weight = draw_forget_weight(jax.random.fold_in(keys[13], 71), 0)
    gate_weight = scatter_about(keys[5], (D, D), D ** -0.5, 0.125, ((0, 16),))
    mixer_gain = jnp.clip(1.0 + 0.15 * jax.random.normal(keys[6], (D,), jnp.float32), 0.25, 1.75).astype(jnp.bfloat16)
    out_weight = scatter_about(keys[7], (D, D), (D // 2) ** -0.5, 0.1875, ((0, 16),))
    ffn_gain = jnp.clip(1.0 + 0.15 * jax.random.normal(keys[8], (D,), jnp.float32), 0.25, 1.75).astype(jnp.bfloat16)
    ffn_gate_weight = scatter_about(keys[9], (D, FF), D ** -0.5, 0.125, ((0, 16),))
    ffn_up_weight = scatter_about(keys[10], (D, FF), D ** -0.5, 0.125, ((0, 16),))
    ffn_down_weight = scatter_about(keys[11], (FF, D), (FF // 4) ** -0.5, 0.15625, ((0, 16),))
    cotangent = scatter_about(keys[12], (SEQS, LEN, D), 1.0, 6.0, ((0, 32),))
    return {"tokens": tokens, "segment_ids": segment_ids, "norm_gain": norm_gain, "input_weight": input_weight, "forget_weight": forget_weight, "gate_weight": gate_weight, "mixer_gain": mixer_gain, "out_weight": out_weight, "ffn_gain": ffn_gain, "ffn_gate_weight": ffn_gate_weight, "ffn_up_weight": ffn_up_weight, "ffn_down_weight": ffn_down_weight, "cotangent": cotangent}


EPSILON = 1e-06
HIGHEST = lax.Precision.HIGHEST

@jax.custom_vjp
def low(v):
    return lax.optimization_barrier(v.astype(jnp.bfloat16)).astype(jnp.float32)

@jax.custom_vjp
def low_back(v):
    return v

def low_keep(v):
    return (low(v), None)

def low_pass(kept, grad):
    return (grad,)

def back_keep(v):
    return (v, None)

def back_low(kept, grad):
    return (low(grad),)
low.defvjp(low_keep, low_pass)
low_back.defvjp(back_keep, back_low)

def product(left, right):
    return jnp.dot(left, right, precision=HIGHEST, preferred_element_type=jnp.float32)

def normalize(values):
    return values * lax.rsqrt(lax.optimization_barrier(jnp.mean(values * values, axis=-1, keepdims=True)) + EPSILON)

def recur(decay, update):

    def advance(carry_state, pair):
        carry_state = pair[0] * carry_state + pair[1]
        return (carry_state, carry_state)
    start = jnp.zeros((decay.shape[1],), jnp.float32)
    return lax.scan(jax.checkpoint(advance), start, (decay, update))[1]

def layer(inputs, segments, weights):
    norm_gain, input_weight, forget_weight, gate_weight, mixer_gain, out_weight, ffn_gain, ffn_gate_weight, ffn_up_weight, ffn_down_weight = weights
    same = jnp.concatenate([jnp.zeros((1,), jnp.float32), (segments[1:] == segments[:-1]).astype(jnp.float32)])
    normed = low(normalize(inputs) * norm_gain)
    input_pre = low_back(product(normed, input_weight))
    forget_pre = low_back(product(normed, forget_weight))
    gate_pre = low_back(product(normed, gate_weight))
    forget = jax.nn.sigmoid(forget_pre)
    update = jax.nn.silu(input_pre) * (1.0 - forget)
    decay = forget * same[:, None]
    state = recur(decay, update)
    mixed = low(normalize(state) * mixer_gain * jax.nn.silu(gate_pre))
    branch = low_back(product(mixed, out_weight))
    resid = inputs + branch
    ffn_in = low(normalize(resid) * ffn_gain)
    ffn_gate = low_back(product(ffn_in, ffn_gate_weight))
    ffn_up = low_back(product(ffn_in, ffn_up_weight))
    hidden = low(jax.nn.silu(ffn_gate) * ffn_up)
    return resid + product(hidden, ffn_down_weight)

def reference(tokens, segment_ids, norm_gain, input_weight, forget_weight, gate_weight, mixer_gain, out_weight, ffn_gain, ffn_gate_weight, ffn_up_weight, ffn_down_weight, cotangent):
    weights = tuple((w.astype(jnp.float32) for w in (norm_gain, input_weight, forget_weight, gate_weight, mixer_gain, out_weight, ffn_gain, ffn_gate_weight, ffn_up_weight, ffn_down_weight)))

    def one_sequence(totals, items):
        inputs, segments, cotangent_row = items
        result, pull = jax.vjp(lambda values, params: layer(values, segments, params), inputs.astype(jnp.float32), weights)
        grad_inputs, grad_weights = pull(cotangent_row.astype(jnp.float32))
        totals = jax.tree.map(lambda left, right: left + right, totals, grad_weights)
        return (totals, (result.astype(jnp.bfloat16), grad_inputs.astype(jnp.bfloat16)))
    zeros = jax.tree.map(jnp.zeros_like, weights)
    totals, outputs = lax.scan(one_sequence, zeros, (tokens, segment_ids, cotangent))
    return (outputs[0], outputs[1], totals[0], totals[1], totals[2], totals[3], totals[4], totals[5], totals[6], totals[7], totals[8], totals[9])
```

```python
import functools

import jax
import jax.numpy as jnp
from jax import lax
from jax.experimental import pallas as pl
from jax.experimental.pallas import tpu as pltpu
from jax.sharding import PartitionSpec as P

EPSILON = 1e-06
AXES = ("rep", "shard")
CORES = 2
F32 = jnp.float32
BF16 = jnp.bfloat16


def normalize(values):
    scale = lax.rsqrt(jnp.mean(values * values, axis=-1, keepdims=True) + EPSILON)
    return (values * scale, scale)


def norm_back(grad_scaled, scaled, scale):
    inner = jnp.mean(grad_scaled * scaled, axis=-1, keepdims=True)
    return scale * (grad_scaled - scaled * inner)


def swish_pair(values):
    sigma = jax.nn.sigmoid(values)
    return (values * sigma, sigma * (1.0 + values * (1.0 - sigma)))


def matmul(left, right, dims, out=F32):
    return lax.dot_general(left, right, ((dims[:1], dims[1:]), ((), ())), preferred_element_type=F32).astype(out)


TILE = 8


def scan_tile(decay, update, reverse):
    row = lax.broadcasted_iota(jnp.int32, decay.shape, 0)
    for step in (1, 2, 4):
        shift = TILE - step if reverse else step
        inside = row < TILE - step if reverse else row >= step
        earlier = jnp.where(inside, pltpu.roll(update, shift, 0), 0.0)
        product = jnp.where(inside, pltpu.roll(decay, shift, 0), 1.0)
        update = update + decay * earlier
        decay = decay * product
    return (decay, update)


def scan_forward_kernel(count, length, decay, update, state):
    def block(step, carries):
        out = []
        for n in range(count):
            rows = pl.ds(pl.multiple_of(n * length + step * TILE, TILE), TILE)
            product, local = scan_tile(decay[rows, :], update[rows, :], False)
            local = local + product * carries[n]
            state[rows, :] = local
            out.append(local[TILE - 1 :, :])
        return tuple(out)

    lax.fori_loop(0, length // TILE, block, (jnp.zeros((1, state.shape[1]), F32),) * count)


def scan_backward_kernel(count, length, decay, grad, carried):
    steps = length // TILE

    def block(step, pairs):
        out = []
        for n in range(count):
            carry, later = pairs[n]
            rows = pl.ds(pl.multiple_of(n * length + (steps - 1 - step) * TILE, TILE), TILE)
            own = decay[rows, :]
            row = lax.broadcasted_iota(jnp.int32, own.shape, 0)
            following = jnp.where(row < TILE - 1, pltpu.roll(own, TILE - 1, 0), later)
            product, local = scan_tile(following, grad[rows, :], True)
            local = local + product * carry
            carried[rows, :] = local
            out.append((local[:1, :], own[:1, :]))
        return tuple(out)

    zero = jnp.zeros((1, carried.shape[1]), F32)
    lax.fori_loop(0, steps, block, ((zero, zero),) * count)


def run_scan(kernel, name, count, length, left, right):
    size = left.size
    return pl.pallas_call(
        functools.partial(kernel, count, length),
        out_shape=jax.ShapeDtypeStruct(left.shape, F32),
        in_specs=[pl.BlockSpec(memory_space=pltpu.VMEM)] * 2,
        out_specs=pl.BlockSpec(memory_space=pltpu.VMEM),
        compiler_params=pltpu.CompilerParams(vmem_limit_bytes=32 * 2**20),
        cost_estimate=pl.CostEstimate(flops=2 * size, bytes_accessed=12 * size, transcendentals=0),
        name=name,
    )(left, right)


class Layout:
    def __init__(self, reps, shards):
        self.reps, self.shards = reps, shards
        self.chips = shards // CORES
        self.outer = 4 if self.chips % 4 == 0 else 1
        self.inner = self.chips // self.outer
        self.r = lax.axis_index("rep")
        place = lax.axis_index("shard")
        self.c = place % CORES
        self.i = (place // CORES) % self.inner
        self.o = place // (CORES * self.inner)
        self.members = reps * CORES

    def send(self, value, dr=0, do=0, di=0, dc=0):
        pairs = []
        for r in range(self.reps):
            for o in range(self.outer):
                for i in range(self.inner):
                    for c in range(CORES):
                        far = ((r + dr) % self.reps, (o + do) % self.outer, (i + di) % self.inner, (c + dc) % CORES)
                        pairs.append((self.number(r, o, i, c), self.number(*far)))
        return lax.ppermute(value, AXES, pairs)

    def number(self, r, o, i, c):
        return ((r * self.outer + o) * self.inner + i) * CORES + c

    def gather_members(self, value):
        both = [value] + [self.send(value, dr=k) for k in range(1, self.reps)]
        rows = jnp.concatenate(both, axis=0)
        return jnp.concatenate([rows, self.send(rows, dc=1)], axis=0)

    def sum_members(self, partial):
        half = partial.shape[0] // CORES
        rows = partial.shape[0] // self.members
        wire = partial.dtype
        total = partial[:half].astype(F32) + self.send(partial[half:], dc=1).astype(F32)
        own = total[:rows]
        for k in range(1, self.reps):
            block = total[k * rows : (k + 1) * rows].astype(wire)
            own = own + self.send(block, dr=-k).astype(F32)
        return own

    def scatter_plane(self, grad):
        rows = grad.shape[0] // self.chips
        grid = grad.reshape(self.outer, self.inner, rows, grad.shape[1])
        pick = lambda k: lax.dynamic_index_in_dim(grid, (self.i + k) % self.inner, 1, keepdims=False)
        total = pick(0).astype(F32)
        for k in range(1, self.inner):
            total = total + self.send(pick(k), di=k).astype(F32)
        line = total.astype(BF16)
        take = lambda k: lax.dynamic_index_in_dim(line, (self.o + k) % self.outer, 0, keepdims=False)
        own = take(0).astype(F32)
        for k in range(1, self.outer):
            own = own + self.send(take(k), do=k).astype(F32)
        return own

    def split_columns(self, weight):
        rows, columns = weight.shape
        small = columns // (self.chips * CORES * self.reps)
        grid = weight.reshape(rows, self.chips, CORES, self.reps, small)
        mine = lax.dynamic_index_in_dim(grid, self.r, 3, keepdims=False)
        return mine.transpose(0, 2, 1, 3).reshape(rows, CORES, self.chips * small)

    def own_columns(self, vector):
        columns = vector.shape[0]
        small = columns // (self.chips * CORES * self.reps)
        grid = vector.reshape(self.chips, CORES, self.reps, small)
        mine = lax.dynamic_index_in_dim(grid, self.c, 1, keepdims=False)
        return lax.dynamic_index_in_dim(mine, self.r, 1, keepdims=False).reshape(-1)

    def join_columns(self, own):
        rows, columns = own.shape[0] // CORES, own.shape[1]
        pair = own.reshape(CORES, rows, columns).astype(BF16)
        mine = lax.dynamic_index_in_dim(pair, self.c, 0, keepdims=False)
        other = self.send(lax.dynamic_index_in_dim(pair, 1 - self.c, 0, keepdims=False), dc=1)
        first = self.c == 0
        cores = jnp.stack([jnp.where(first, mine, other), jnp.where(first, other, mine)])
        return self.join_reps(cores)

    def join_reps(self, value):
        parts = [value] + [self.send(value, dr=k) for k in range(1, self.reps)]
        if self.reps == 2:
            first = self.r == 0
            return jnp.stack([jnp.where(first, parts[0], parts[1]), jnp.where(first, parts[1], parts[0])])
        stacked = jnp.stack(parts[::-1] + parts[::-1])
        return lax.dynamic_slice_in_dim(stacked, self.reps - 1 - self.r, self.reps, 0)

    def natural(self, joined):
        reps, cores, rows, columns = joined.shape
        small = columns // self.chips
        grid = joined.reshape(reps, cores, rows, self.chips, small).transpose(2, 3, 1, 0, 4)
        return grid.reshape(rows, self.chips * cores * reps * small).astype(F32)


def shards(
    reps,
    places,
    tokens,
    segment_ids,
    norm_gain,
    input_weight,
    forget_weight,
    gate_weight,
    mixer_gain,
    out_weight,
    ffn_gain,
    ffn_gate_weight,
    ffn_up_weight,
    ffn_down_weight,
    cotangent,
):
    at = Layout(reps, places)
    inputs = tokens[0].astype(F32)
    length, width = inputs.shape
    units = ffn_up_weight.shape[1]
    channels = width // at.members
    part = units // at.members
    count = at.members

    mix_local = jnp.stack([at.split_columns(w) for w in (input_weight, forget_weight, gate_weight)], axis=2)
    mix_local = mix_local.reshape(mix_local.shape[0], -1)
    pair_local = jnp.stack([at.split_columns(w) for w in (ffn_gate_weight, ffn_up_weight)], axis=2)
    pair_local = pair_local.reshape(pair_local.shape[0], -1)
    rep_rows = lambda w: lax.dynamic_index_in_dim(w.reshape(reps, w.shape[0] // reps, w.shape[1]), at.r, 0, keepdims=False)
    gather = lambda w: lax.all_gather(w, "shard", axis=0, tiled=True)
    core_columns = lambda w: lax.dynamic_index_in_dim(w.reshape(w.shape[0], CORES, -1), at.c, 1, keepdims=False)
    core_rows = lambda w, n: lax.dynamic_index_in_dim(w.reshape(at.chips, CORES, n, w.shape[1]), at.c, 1, keepdims=False).reshape(-1, w.shape[1])
    gains = lax.all_gather(jnp.stack([norm_gain, mixer_gain, ffn_gain]), "shard", axis=1, tiled=True).astype(F32)
    gain_one, gain_two, gain_three = gains[0], gains[1], gains[2]
    mix_weight = core_columns(gather(mix_local))
    out_rows = core_rows(gather(rep_rows(out_weight)), out_weight.shape[0] // reps)
    pair_weight = core_columns(gather(pair_local))
    down_rows = core_rows(gather(rep_rows(ffn_down_weight)), ffn_down_weight.shape[0] // reps)

    grad_out = cotangent[0]
    all_grad_out = at.gather_members(grad_out)
    segments = at.gather_members(segment_ids)
    starts = jnp.zeros((count, 1), F32)
    same = jnp.concatenate([starts, (segments[:, 1:] == segments[:, :-1]).astype(F32)], axis=1)
    same = same.reshape(count * length, 1)
    scaled_in, scale_in = normalize(inputs)
    normed = at.gather_members((scaled_in * gain_one).astype(BF16))
    pre = matmul(normed, mix_weight, (1, 0))
    input_pre, forget_pre, gate_pre = (pre[:, k * channels : (k + 1) * channels] for k in range(3))
    forget = jax.nn.sigmoid(forget_pre)
    input_act, input_slope = swish_pair(input_pre)
    decay = forget * same
    state = run_scan(scan_forward_kernel, "scan_forward", count, length, decay, input_act * (1.0 - forget))
    gate_act, gate_slope = swish_pair(gate_pre)
    gain_mix = at.own_columns(gain_two)
    mixed_raw = (state * gain_mix * gate_act).astype(BF16)
    squares = jnp.sum(state * state, axis=1).reshape(count, length)
    square_sum = at.sum_members(squares)
    branch_sum = at.sum_members(matmul(mixed_raw, out_rows, (1, 0), BF16))
    state_scale = lax.rsqrt(square_sum / width + EPSILON)
    branch = branch_sum * state_scale.reshape(length, 1)
    resid = inputs + branch

    scaled_mid, scale_mid = normalize(resid)
    ffn_in = at.gather_members((scaled_mid * gain_three).astype(BF16))
    pair = matmul(ffn_in, pair_weight, (1, 0))
    ffn_gate, ffn_up = pair[:, :part], pair[:, part:]
    ffn_act, ffn_slope = swish_pair(ffn_gate)
    hidden = (ffn_act * ffn_up).astype(BF16)
    down_grad = at.scatter_plane(matmul(hidden, all_grad_out, (0, 0), BF16))
    ffn_out = at.sum_members(matmul(hidden, down_rows, (1, 0), BF16))
    block_output = (resid + ffn_out).astype(BF16)
    grad_hidden = matmul(all_grad_out, down_rows, (1, 1))
    grad_fgate = (grad_hidden * ffn_up * ffn_slope).astype(BF16)
    grad_fup = (grad_hidden * ffn_act).astype(BF16)
    grad_pair = jnp.concatenate([grad_fgate, grad_fup], axis=1)
    grad_ffn_in = at.sum_members(matmul(grad_pair, pair_weight, (1, 1), BF16))
    gate_grad = at.scatter_plane(matmul(ffn_in, grad_fgate, (0, 0), BF16))
    up_grad = at.scatter_plane(matmul(ffn_in, grad_fup, (0, 0), BF16))
    grad_resid = grad_out.astype(F32) + norm_back(grad_ffn_in * gain_three, scaled_mid, scale_mid)
    grad_branch_own = grad_resid.astype(BF16)

    grad_branch = at.gather_members(grad_branch_own)
    inner_own = jnp.mean(grad_branch_own.astype(F32) * branch, axis=1)
    row_facts = at.gather_members(jnp.stack([state_scale.reshape(length), inner_own])[None])
    all_scale = row_facts[:, 0].reshape(count * length, 1)
    all_inner = row_facts[:, 1].reshape(count * length, 1)
    state_scaled = state * all_scale
    mixed = (state_scaled * gain_mix * gate_act).astype(BF16)
    weighted = matmul(grad_branch, out_rows, (1, 1)) * gain_mix
    out_grad = at.scatter_plane(matmul(mixed, grad_branch, (0, 0), BF16))
    grad_gate_pre = (weighted * state_scaled * gate_slope).astype(BF16)
    grad_state = all_scale * (weighted * gate_act - state_scaled * all_inner)
    carried = run_scan(scan_backward_kernel, "scan_backward", count, length, decay, grad_state)
    line = state.reshape(count, length, channels)
    previous = jnp.concatenate([jnp.zeros((count, 1, channels), F32), line[:, :-1]], axis=1).reshape(state.shape)
    grad_forget = carried * previous * same - carried * input_act
    grad_input_pre = (carried * (1.0 - forget) * input_slope).astype(BF16)
    grad_forget_pre = (grad_forget * forget * (1.0 - forget)).astype(BF16)
    triple = jnp.concatenate([grad_input_pre, grad_forget_pre, grad_gate_pre], axis=1)
    grad_normed = at.sum_members(matmul(triple, mix_weight, (1, 1), BF16))
    mix_grads = [at.scatter_plane(matmul(normed, g, (0, 0), BF16)) for g in (grad_input_pre, grad_forget_pre, grad_gate_pre)]
    input_grad = (grad_resid + norm_back(grad_normed * gain_one, scaled_in, scale_in)).astype(BF16)

    whole = lambda own: at.natural(at.join_columns(own))
    stacked = lambda own: at.join_reps(own.astype(BF16)).reshape(-1, own.shape[1]).astype(F32)
    down_total = stacked(down_grad)
    gate_total, up_total = whole(gate_grad), whole(up_grad)
    out_total = stacked(out_grad)
    mix_totals = [whole(g) for g in mix_grads]
    dotted = lambda w, g: jnp.sum(w.astype(F32) * g, axis=1)
    norm_gain_grad = sum(dotted(w, g) for w, g in zip((input_weight, forget_weight, gate_weight), mix_totals)) / norm_gain.astype(F32)
    mixer_gain_grad = dotted(out_weight, out_total) / mixer_gain.astype(F32)
    ffn_gain_grad = (dotted(ffn_gate_weight, gate_total) + dotted(ffn_up_weight, up_total)) / ffn_gain.astype(F32)
    return (
        block_output[None],
        input_grad[None],
        norm_gain_grad,
        *mix_totals,
        mixer_gain_grad,
        out_total,
        ffn_gain_grad,
        gate_total,
        up_total,
        down_total,
    )


def solution(mesh):
    tokens, vector, matrix = P(AXES, None, None), P("shard"), P("shard", None)
    placed = (tokens, P(AXES, None), vector, matrix, matrix, matrix, vector, matrix, vector, matrix, matrix, matrix, tokens)
    return jax.shard_map(
        functools.partial(shards, mesh.shape["rep"], mesh.shape["shard"]),
        mesh=mesh,
        in_specs=placed,
        out_specs=(tokens, tokens, vector, matrix, matrix, matrix, vector, matrix, vector, matrix, matrix, matrix),
        check_vma=False,
    )
```

```python
import functools

import jax
import jax.numpy as jnp
from jax import lax
from jax.experimental import pallas as pl
from jax.experimental.pallas import tpu as pltpu
from jax.sharding import PartitionSpec as P

EPSILON = 1e-06
AXES = ("rep", "shard")
CORES = 2
F32 = jnp.float32
BF16 = jnp.bfloat16


def normalize(values):
    scale = lax.rsqrt(jnp.mean(values * values, axis=-1, keepdims=True) + EPSILON)
    return (values * scale, scale)


def norm_back(grad_scaled, scaled, scale):
    inner = jnp.mean(grad_scaled * scaled, axis=-1, keepdims=True)
    return scale * (grad_scaled - scaled * inner)


def swish_pair(values):
    sigma = jax.nn.sigmoid(values)
    return (values * sigma, sigma * (1.0 + values * (1.0 - sigma)))


def matmul(left, right, dims, out=F32):
    return lax.dot_general(left, right, ((dims[:1], dims[1:]), ((), ())), preferred_element_type=F32).astype(out)


TILE = 8


def scan_tile(decay, update, reverse):
    row = lax.broadcasted_iota(jnp.int32, decay.shape, 0)
    for step in (1, 2, 4):
        shift = TILE - step if reverse else step
        inside = row < TILE - step if reverse else row >= step
        earlier = jnp.where(inside, pltpu.roll(update, shift, 0), 0.0)
        product = jnp.where(inside, pltpu.roll(decay, shift, 0), 1.0)
        update = update + decay * earlier
        decay = decay * product
    return (decay, update)


def scan_forward_kernel(count, length, decay, update, state):
    def block(step, carries):
        out = []
        for n in range(count):
            rows = pl.ds(pl.multiple_of(n * length + step * TILE, TILE), TILE)
            product, local = scan_tile(decay[rows, :], update[rows, :], False)
            local = local + product * carries[n]
            state[rows, :] = local
            out.append(local[TILE - 1 :, :])
        return tuple(out)

    lax.fori_loop(0, length // TILE, block, (jnp.zeros((1, state.shape[1]), F32),) * count)


def scan_backward_kernel(count, length, decay, grad, carried):
    steps = length // TILE

    def block(step, pairs):
        out = []
        for n in range(count):
            carry, later = pairs[n]
            rows = pl.ds(pl.multiple_of(n * length + (steps - 1 - step) * TILE, TILE), TILE)
            own = decay[rows, :]
            row = lax.broadcasted_iota(jnp.int32, own.shape, 0)
            following = jnp.where(row < TILE - 1, pltpu.roll(own, TILE - 1, 0), later)
            product, local = scan_tile(following, grad[rows, :], True)
            local = local + product * carry
            carried[rows, :] = local
            out.append((local[:1, :], own[:1, :]))
        return tuple(out)

    zero = jnp.zeros((1, carried.shape[1]), F32)
    lax.fori_loop(0, steps, block, ((zero, zero),) * count)


def run_scan(kernel, name, count, length, left, right):
    size = left.size
    return pl.pallas_call(
        functools.partial(kernel, count, length),
        out_shape=jax.ShapeDtypeStruct(left.shape, F32),
        in_specs=[pl.BlockSpec(memory_space=pltpu.VMEM)] * 2,
        out_specs=pl.BlockSpec(memory_space=pltpu.VMEM),
        compiler_params=pltpu.CompilerParams(vmem_limit_bytes=32 * 2**20),
        cost_estimate=pl.CostEstimate(flops=2 * size, bytes_accessed=12 * size, transcendentals=0),
        name=name,
    )(left, right)


def move_kernel(blocks, source, value, out):
    wide = value.shape[1] // blocks
    for k in range(blocks):
        out[:, k * wide : (k + 1) * wide] = value[:, pl.ds(pl.multiple_of(source[k] * wide, 128), wide)]


def move_blocks(source, value):
    return pl.pallas_call(
        functools.partial(move_kernel, source.shape[0]),
        out_shape=jax.ShapeDtypeStruct(value.shape, value.dtype),
        in_specs=[pl.BlockSpec(memory_space=pltpu.SMEM), pl.BlockSpec(memory_space=pltpu.VMEM)],
        out_specs=pl.BlockSpec(memory_space=pltpu.VMEM),
        cost_estimate=pl.CostEstimate(flops=0, bytes_accessed=2 * value.size * value.dtype.itemsize, transcendentals=0),
        name="move_blocks",
    )(source, value)


class Place:
    def __init__(self, reps, shards):
        self.reps, self.shards = reps, shards
        self.chips = shards // CORES
        self.hi = self.chips // 4
        self.r = lax.axis_index("rep")
        self.s = lax.axis_index("shard")
        self.c = self.s % CORES
        self.core = ("shard", 1)
        self.low = ("shard", 2)
        self.lo = ("shard", 4)
        self.his = [("shard", 8 << k) for k in range(self.hi.bit_length() - 1)]
        self.rep_bits = [("rep", 1 << k) for k in range(reps.bit_length() - 1)]
        self.mixers = self.rep_bits + [self.core]
        self.feeders = self.rep_bits + [self.lo, self.core]

    def bit(self, which):
        axis, value = which
        return ((self.r if axis == "rep" else self.s) // value) % 2

    def swap(self, value, which):
        axis, flip = which
        flip = flip * self.shards if axis == "rep" else flip
        return lax.ppermute(value, AXES, [(n, n ^ flip) for n in range(self.reps * self.shards)])

    def merge(self, own, other, which, axis=0):
        first = self.bit(which) == 0
        return jnp.stack([jnp.where(first, own, other), jnp.where(first, other, own)], axis)

    def join(self, value, which, axis=0):
        return self.merge(value, self.swap(value, which), which, axis)

    def pick(self, value, which, axis, flipped=False):
        bit = self.bit(which)
        return lax.dynamic_index_in_dim(value, 1 - bit if flipped else bit, axis, keepdims=False)

    def trade(self, value, which, axis):
        other = self.swap(self.pick(value, which, axis, True), which)
        return self.merge(self.pick(value, which, axis), other, which)

    def reduce(self, value, which, axis):
        other = self.swap(self.pick(value, which, axis, True), which)
        return (self.pick(value, which, axis).astype(F32) + other.astype(F32)).astype(BF16)

    def extend(self, value, which):
        return jnp.concatenate([value, self.swap(value, which)], axis=0)

    def fold(self, value, which):
        half = value.shape[0] // 2
        other = self.swap(value[half:], which)
        return (value[:half].astype(F32) + other.astype(F32)).astype(BF16)

    def block_order(self, value, back=False):
        place = jnp.arange(self.chips, dtype=jnp.int32)
        here = self.s // CORES
        if back:
            other = place ^ (here & ~2)
            source = (other & 1) * (2 * self.hi) + (other >> 1)
        else:
            chip = (place % (2 * self.hi)) * 2 + place // (2 * self.hi)
            source = chip ^ (here & ~2)
        return move_blocks(source, value)

    def gather_members(self, value, bits):
        for which in bits:
            value = jnp.concatenate([value, self.swap(value, which)], axis=0)
        return value

    def sum_members(self, partial, bits):
        wire, total = partial.dtype, partial
        for which in bits[::-1]:
            half = total.shape[0] // 2
            total = total[:half].astype(F32) + self.swap(total[half:].astype(wire), which).astype(F32)
        return total

    def join_his(self, value):
        for which in self.his:
            value = self.join(value, which)
        return value.reshape((self.hi,) + value.shape[len(self.his) :])

    def reduce_his(self, value):
        value = value.reshape((2,) * len(self.his) + value.shape[1:])
        for which in self.his[::-1]:
            value = self.reduce(value, which, 0)
        return value

    def join_reps(self, value):
        for which in self.rep_bits:
            value = self.join(value, which)
        return value.reshape((self.reps,) + value.shape[len(self.rep_bits) :])

    def own_rep(self, weight):
        return lax.dynamic_index_in_dim(weight.reshape(self.reps, -1, weight.shape[1]), self.r, 0, keepdims=False)

    def groups(self, bits):
        flips = [value * self.shards if axis == "rep" else value for axis, value in bits]
        group = [0]
        for flip in flips:
            group = group + [n + flip for n in group]
        group = sorted(group)
        return [[base + n for n in group] for base in range(self.reps * self.shards) if not base & sum(flips)]

    def gather_group(self, value):
        return lax.all_gather(value, AXES, axis=0, tiled=True, axis_index_groups=self.groups(self.feeders))

    def sum_group(self, value):
        return lax.psum_scatter(value, AXES, scatter_dimension=0, tiled=True, axis_index_groups=self.groups(self.feeders)).astype(F32)


def fence(*values):
    return lax.optimization_barrier(values)


def late(value, *others):
    return fence(value, *others)[0]


def chooser(sources, targets, source_of):
    row = lax.broadcasted_iota(jnp.int32, (sources, targets), 0)
    column = lax.broadcasted_iota(jnp.int32, (sources, targets), 1)
    return (row == source_of(column)).astype(BF16)


def shards(
    reps,
    places,
    tokens,
    segment_ids,
    norm_gain,
    input_weight,
    forget_weight,
    gate_weight,
    mixer_gain,
    out_weight,
    ffn_gain,
    ffn_gate_weight,
    ffn_up_weight,
    ffn_down_weight,
    cotangent,
):
    at = Place(reps, places)
    inputs = tokens[0].astype(F32)
    length, width = inputs.shape
    units = ffn_up_weight.shape[1]
    count = 2 ** len(at.mixers)
    channels = width // count
    part = units // 2 ** len(at.feeders)
    rows = width // places
    small = rows // reps
    slim = units // (places * reps)
    chip_rows = CORES * rows

    def channel_source(position):
        core, chip, inner = position // channels, position % channels // small, position % small
        return ((chip * CORES + core) * reps + at.r) * small + inner

    triple_rows = jnp.concatenate([input_weight, forget_weight, gate_weight])
    picked = matmul(triple_rows, chooser(width, CORES * channels, channel_source), (1, 0), BF16)
    picked = picked.reshape(3, rows, CORES, channels).transpose(1, 2, 0, 3).reshape(rows, -1)
    mix_all = lax.all_gather(picked, "shard", axis=0, tiled=True)

    def unit_source(core):
        def source(position):
            hi, low, inner = position // (2 * slim), position % (2 * slim) // slim, position % slim
            return hi * (units // (2 * at.hi)) + ((low * CORES + core) * reps + at.r) * slim + inner

        return source

    pair_rows = jnp.concatenate([ffn_gate_weight, ffn_up_weight])
    strip = units // (2 * at.hi)
    strips = [pair_rows[:, k * strip : (k + 1) * strip] for k in range(2 * at.hi)]
    pair_lines = jnp.concatenate([jnp.concatenate(strips[k::2], axis=1) for k in range(2)])
    pick_units = lambda core: matmul(pair_lines, chooser(units // 2, part, unit_source(core)), (1, 0), BF16)
    kept, given = pick_units(at.c), pick_units(1 - at.c)

    grad_out = cotangent[0]
    all_tokens = at.gather_members(tokens[0], at.mixers)
    segments = at.gather_members(segment_ids, at.mixers)
    starts = jnp.zeros((count, 1), F32)
    same = jnp.concatenate([starts, (segments[:, 1:] == segments[:, :-1]).astype(F32)], axis=1)
    same = same.reshape(count * length, 1)
    out_rows = at.join(at.join_his(at.join(at.own_rep(out_weight), at.lo)), at.low, 2).reshape(channels, width)
    gains = lax.all_gather(jnp.stack([norm_gain, mixer_gain, ffn_gain]), "shard", axis=1, tiled=True).astype(F32)
    gain_one, gain_two, gain_three = gains[0], gains[1], gains[2]
    gain_grid = gain_two.reshape(at.chips, CORES, reps, small)
    gain_mix = lax.dynamic_index_in_dim(lax.dynamic_index_in_dim(gain_grid, at.c, 1, keepdims=False), at.r, 1, keepdims=False).reshape(-1)
    normed = (normalize(all_tokens.astype(F32))[0] * gain_one).astype(BF16)
    lines = lambda value: value.reshape(2 * CORES, rows, part)
    chip = at.merge(lines(kept), lines(at.swap(given, at.core)), at.core, 1).reshape(2, CORES * chip_rows, part)
    mix_all, normed, same, chip, out_rows, grad_out_sent, own_down = fence(
        mix_all, normed, same, chip, out_rows, grad_out, at.own_rep(ffn_down_weight)
    )

    all_grad_out = at.gather_group(grad_out_sent)
    own_pair = at.trade(chip, at.lo, 0)
    mix_weight = lax.dynamic_slice_in_dim(mix_all, at.c * (3 * channels), 3 * channels, 1)
    pre = matmul(normed, mix_weight, (1, 0))
    input_pre, forget_pre, gate_pre = (pre[:, k * channels : (k + 1) * channels] for k in range(3))
    forget = jax.nn.sigmoid(forget_pre)
    input_act, input_slope = swish_pair(input_pre)
    decay = forget * same
    state = run_scan(scan_forward_kernel, "scan_forward", count, length, decay, input_act * (1.0 - forget))
    gate_act, gate_slope = swish_pair(gate_pre)
    mixed_raw = (state * gain_mix * gate_act).astype(BF16)
    squares = jnp.sum(state * state, axis=1).reshape(count, length)
    out_part, squares, own_pair = fence(matmul(mixed_raw, out_rows, (1, 0), BF16), squares, own_pair)

    pair_grid = own_pair.reshape(2, 2, chip_rows, part)
    gate_half, up_half = pair_grid[:, 0].reshape(-1, part), pair_grid[:, 1].reshape(-1, part)
    for which in at.his:
        gate_half = at.extend(gate_half, which)
    square_sum = at.sum_members(squares, at.mixers)
    branch_sum = at.sum_members(out_part, at.mixers)
    branch_sum, square_sum, gate_half, up_half = fence(branch_sum, square_sum, gate_half, up_half)

    gate_columns = at.extend(gate_half, at.low)
    for which in at.his:
        up_half = at.extend(up_half, which)
    state_scale = lax.rsqrt(square_sum / width + EPSILON)
    branch = branch_sum * state_scale.reshape(length, 1)
    resid = inputs + branch
    scaled_mid, scale_mid = normalize(resid)
    ffn_in = at.gather_group(at.block_order((scaled_mid * gain_three).astype(BF16)))
    ffn_in, gate_columns, up_half, own_down, all_grad_out = fence(ffn_in, gate_columns, up_half, own_down, all_grad_out)
    up_columns = at.extend(up_half, at.low)
    down_lines = at.join_his(own_down)
    ffn_gate = matmul(ffn_in, gate_columns, (1, 0))
    ffn_gate, up_columns, down_lines, ffn_in = fence(ffn_gate, up_columns, down_lines, ffn_in)
    down_rows = at.join(down_lines, at.low, 1).reshape(part, width)
    ffn_up = matmul(ffn_in, up_columns, (1, 0))
    ffn_act, ffn_slope = swish_pair(ffn_gate)
    hidden = (ffn_act * ffn_up).astype(BF16)
    down_cut = matmul(hidden, all_grad_out, (0, 0), BF16)
    down_rows, down_cut, hidden = fence(down_rows, down_cut, hidden)
    down_grid = down_cut.reshape(at.hi, 2, -1, width)
    down_line = at.reduce(down_grid, at.low, 1)
    grad_hidden = matmul(all_grad_out, down_rows, (1, 1))
    grad_fgate = (grad_hidden * ffn_up * ffn_slope).astype(BF16)
    grad_fup = (grad_hidden * ffn_act).astype(BF16)
    grad_cut = (matmul(grad_fgate, gate_columns, (1, 1)) + matmul(grad_fup, up_columns, (1, 1))).astype(BF16)
    grad_cut, grad_fgate, grad_fup = fence(grad_cut, grad_fgate, grad_fup)

    grad_ffn_in = at.sum_group(grad_cut)
    gate_cut = matmul(ffn_in, grad_fgate, (0, 0), BF16)
    up_cut = matmul(ffn_in, grad_fup, (0, 0), BF16)
    ffn_part = matmul(hidden, down_rows, (1, 0), BF16)
    gate_line = at.fold(gate_cut, at.low)
    grad_ffn_in, gate_line, down_line, ffn_part, up_cut = fence(grad_ffn_in, gate_line, down_line, ffn_part, up_cut)
    up_line = at.fold(up_cut, at.low)
    down_own = at.reduce_his(down_line)
    grad_ffn_in = at.block_order(grad_ffn_in.astype(BF16), True).astype(F32)
    grad_resid = grad_out.astype(F32) + norm_back(grad_ffn_in * gain_three, scaled_mid, scale_mid)
    grad_branch_own = grad_resid.astype(BF16)
    inner_own = jnp.mean(grad_branch_own.astype(F32) * branch, axis=1)
    row_facts = at.gather_members(jnp.stack([state_scale.reshape(length), inner_own])[None], at.mixers)
    grad_branch = at.gather_members(grad_branch_own, at.mixers)
    grad_branch, row_facts, down_own, up_line, ffn_part, gate_line = fence(grad_branch, row_facts, down_own, up_line, ffn_part, gate_line)

    all_scale = row_facts[:, 0].reshape(count * length, 1)
    all_inner = row_facts[:, 1].reshape(count * length, 1)
    state_scaled = state * all_scale
    mixed = (state_scaled * gain_mix * gate_act).astype(BF16)
    weighted = matmul(grad_branch, out_rows, (1, 1)) * gain_mix

    def plane_grad(left, right, own_rows):
        cut = matmul(left, right, (0, 0), BF16).reshape(at.hi, 2, 2, own_rows, -1)
        return at.reduce(at.reduce_his(at.reduce(cut, at.low, 2)), at.lo, 0)

    out_own = plane_grad(mixed, grad_branch, small)
    grad_gate_pre = (weighted * state_scaled * gate_slope).astype(BF16)
    grad_state = all_scale * (weighted * gate_act - state_scaled * all_inner)
    carried = run_scan(scan_backward_kernel, "scan_backward", count, length, decay, grad_state)
    line = state.reshape(count, length, channels)
    previous = jnp.concatenate([jnp.zeros((count, 1, channels), F32), line[:, :-1]], axis=1).reshape(state.shape)
    grad_forget = carried * previous * same - carried * input_act
    grad_input_pre = (carried * (1.0 - forget) * input_slope).astype(BF16)
    grad_forget_pre = (grad_forget * forget * (1.0 - forget)).astype(BF16)
    triple = jnp.concatenate([grad_input_pre, grad_forget_pre, grad_gate_pre], axis=1)
    grad_normed = at.sum_members(matmul(triple, mix_weight, (1, 1), BF16), at.mixers)

    def channel_grad(right):
        return at.trade(plane_grad(normed, right, chip_rows).reshape(CORES, rows, channels), at.core, 0)

    mix_owns = [channel_grad(g) for g in (grad_input_pre, grad_forget_pre, grad_gate_pre)]

    def unit_grad(lines):
        for which in at.his[::-1]:
            lines = at.fold(lines, which)
        sets = at.trade(lines.reshape(2, chip_rows, part), at.lo, 0)
        return at.trade(sets.reshape(2, CORES, rows, part), at.core, 1)

    gate_own, up_own = unit_grad(gate_line), unit_grad(up_line)
    ffn_out = late(at.sum_group(ffn_part), triple)
    block_output = (resid + ffn_out).astype(BF16)
    scaled_in, scale_in = normalize(inputs)
    input_grad = (grad_resid + norm_back(grad_normed * gain_one, scaled_in, scale_in)).astype(BF16)

    def channel_place(column):
        chip, core = column // (CORES * reps * small), column // (reps * small) % CORES
        return ((column // small % reps * CORES + core) * at.chips + chip) * small + column % small

    def whole_channels(owns):
        joined = jnp.stack([at.join_reps(own) for own in owns])
        lines = joined.reshape(len(owns), reps * CORES, rows, channels).transpose(0, 2, 1, 3).reshape(-1, width)
        return jnp.split(matmul(lines, chooser(width, width, channel_place), (1, 0)), len(owns))

    def whole_units(own):
        grid = at.join_reps(own).reshape(reps, CORES, 2, rows, at.hi, 2, slim)
        return grid.transpose(3, 4, 2, 5, 1, 0, 6).reshape(rows, units).astype(F32)

    def whole_rows(own):
        return at.join_reps(own).reshape(-1, width).astype(F32)

    down_total = whole_rows(down_own)
    gate_total, up_total = whole_units(gate_own), whole_units(up_own)
    out_total = whole_rows(out_own)
    mix_totals = whole_channels(mix_owns)
    dotted = lambda w, g: jnp.sum(w.astype(F32) * g, axis=1)
    norm_gain_grad = sum(dotted(w, g) for w, g in zip((input_weight, forget_weight, gate_weight), mix_totals)) / norm_gain.astype(F32)
    mixer_gain_grad = dotted(out_weight, out_total) / mixer_gain.astype(F32)
    ffn_gain_grad = (dotted(ffn_gate_weight, gate_total) + dotted(ffn_up_weight, up_total)) / ffn_gain.astype(F32)
    return (
        block_output[None],
        input_grad[None],
        norm_gain_grad,
        *mix_totals,
        mixer_gain_grad,
        out_total,
        ffn_gain_grad,
        gate_total,
        up_total,
        down_total,
    )


def solution(mesh):
    tokens, vector, matrix = P(AXES, None, None), P("shard"), P("shard", None)
    placed = (tokens, P(AXES, None), vector, matrix, matrix, matrix, vector, matrix, vector, matrix, matrix, matrix, tokens)
    return jax.shard_map(
        functools.partial(shards, mesh.shape["rep"], mesh.shape["shard"]),
        mesh=mesh,
        in_specs=placed,
        out_specs=(tokens, tokens, vector, matrix, matrix, matrix, vector, matrix, vector, matrix, matrix, matrix),
        check_vma=False,
    )
```

```python
import functools

import jax
import jax.numpy as jnp
from jax import lax
from jax.experimental import pallas as pl
from jax.experimental.pallas import tpu as pltpu
from jax.sharding import PartitionSpec as P

EPSILON = 1e-06
AXES = ("rep", "shard")
CORES = 2
F32 = jnp.float32
BF16 = jnp.bfloat16


def normalize(values):
    scale = lax.rsqrt(jnp.mean(values * values, axis=-1, keepdims=True) + EPSILON)
    return (values * scale, scale)


def norm_back(grad_scaled, scaled, scale):
    inner = jnp.mean(grad_scaled * scaled, axis=-1, keepdims=True)
    return scale * (grad_scaled - scaled * inner)


def swish_pair(values):
    sigma = jax.nn.sigmoid(values)
    return (values * sigma, sigma * (1.0 + values * (1.0 - sigma)))


def matmul(left, right, dims, out=F32):
    return lax.dot_general(left, right, ((dims[:1], dims[1:]), ((), ())), preferred_element_type=F32).astype(out)


TILE = 8


def scan_tile(decay, update, reverse):
    row = lax.broadcasted_iota(jnp.int32, decay.shape, 0)
    for step in (1, 2, 4):
        shift = TILE - step if reverse else step
        inside = row < TILE - step if reverse else row >= step
        earlier = jnp.where(inside, pltpu.roll(update, shift, 0), 0.0)
        product = jnp.where(inside, pltpu.roll(decay, shift, 0), 1.0)
        update = update + decay * earlier
        decay = decay * product
    return (decay, update)


def scan_forward_kernel(count, length, decay, update, state):
    def block(step, carries):
        out = []
        for n in range(count):
            rows = pl.ds(pl.multiple_of(n * length + step * TILE, TILE), TILE)
            product, local = scan_tile(decay[rows, :], update[rows, :], False)
            local = local + product * carries[n]
            state[rows, :] = local
            out.append(local[TILE - 1 :, :])
        return tuple(out)

    lax.fori_loop(0, length // TILE, block, (jnp.zeros((1, state.shape[1]), F32),) * count)


def scan_backward_kernel(count, length, decay, grad, carried):
    steps = length // TILE

    def block(step, pairs):
        out = []
        for n in range(count):
            carry, later = pairs[n]
            rows = pl.ds(pl.multiple_of(n * length + (steps - 1 - step) * TILE, TILE), TILE)
            own = decay[rows, :]
            row = lax.broadcasted_iota(jnp.int32, own.shape, 0)
            following = jnp.where(row < TILE - 1, pltpu.roll(own, TILE - 1, 0), later)
            product, local = scan_tile(following, grad[rows, :], True)
            local = local + product * carry
            carried[rows, :] = local
            out.append((local[:1, :], own[:1, :]))
        return tuple(out)

    zero = jnp.zeros((1, carried.shape[1]), F32)
    lax.fori_loop(0, steps, block, ((zero, zero),) * count)


def run_scan(kernel, name, count, length, left, right):
    size = left.size
    return pl.pallas_call(
        functools.partial(kernel, count, length),
        out_shape=jax.ShapeDtypeStruct(left.shape, F32),
        in_specs=[pl.BlockSpec(memory_space=pltpu.VMEM)] * 2,
        out_specs=pl.BlockSpec(memory_space=pltpu.VMEM),
        compiler_params=pltpu.CompilerParams(vmem_limit_bytes=32 * 2**20),
        cost_estimate=pl.CostEstimate(flops=2 * size, bytes_accessed=12 * size, transcendentals=0),
        name=name,
    )(left, right)


def move_kernel(blocks, source, value, out):
    wide = value.shape[1] // blocks
    for k in range(blocks):
        out[:, k * wide : (k + 1) * wide] = value[:, pl.ds(pl.multiple_of(source[k] * wide, 128), wide)]


def move_blocks(source, value):
    return pl.pallas_call(
        functools.partial(move_kernel, source.shape[0]),
        out_shape=jax.ShapeDtypeStruct(value.shape, value.dtype),
        in_specs=[pl.BlockSpec(memory_space=pltpu.SMEM), pl.BlockSpec(memory_space=pltpu.VMEM)],
        out_specs=pl.BlockSpec(memory_space=pltpu.VMEM),
        cost_estimate=pl.CostEstimate(flops=0, bytes_accessed=2 * value.size * value.dtype.itemsize, transcendentals=0),
        name="move_blocks",
    )(source, value)


class Place:
    def __init__(self, reps, shards):
        self.reps, self.shards = reps, shards
        self.chips = shards // CORES
        self.hi = self.chips // 4
        self.length = self.chips // 2
        self.r = lax.axis_index("rep")
        self.s = lax.axis_index("shard")
        self.c = self.s % CORES
        self.core = ("shard", 1)
        self.low = ("shard", 2)
        self.lo = ("shard", 4)
        self.his = [("shard", 8 << k) for k in range(self.hi.bit_length() - 1)]
        self.rep_bits = [("rep", 1 << k) for k in range(reps.bit_length() - 1)]
        self.mixers = self.rep_bits + [self.core]
        self.feeders = self.rep_bits + [self.low, self.core]

    def bit(self, which):
        axis, value = which
        return ((self.r if axis == "rep" else self.s) // value) % 2

    def swap(self, value, which):
        axis, flip = which
        flip = flip * self.shards if axis == "rep" else flip
        return lax.ppermute(value, AXES, [(n, n ^ flip) for n in range(self.reps * self.shards)])

    def merge(self, own, other, which, axis=0):
        first = self.bit(which) == 0
        return jnp.stack([jnp.where(first, own, other), jnp.where(first, other, own)], axis)

    def join(self, value, which, axis=0):
        return self.merge(value, self.swap(value, which), which, axis)

    def pick(self, value, which, axis, flipped=False):
        bit = self.bit(which)
        return lax.dynamic_index_in_dim(value, 1 - bit if flipped else bit, axis, keepdims=False)

    def trade(self, value, which, axis):
        other = self.swap(self.pick(value, which, axis, True), which)
        return self.merge(self.pick(value, which, axis), other, which)

    def reduce(self, value, which, axis):
        other = self.swap(self.pick(value, which, axis, True), which)
        return (self.pick(value, which, axis).astype(F32) + other.astype(F32)).astype(BF16)

    def begin(self, value, which, axis):
        return (self.pick(value, which, axis), self.swap(self.pick(value, which, axis, True), which))

    def end(self, own, other):
        return (own.astype(F32) + other.astype(F32)).astype(BF16)

    def extend(self, value, which):
        return jnp.concatenate([value, self.swap(value, which)], axis=0)

    def fold(self, value, which):
        half = value.shape[0] // 2
        other = self.swap(value[half:], which)
        return (value[:half].astype(F32) + other.astype(F32)).astype(BF16)

    def block_order(self, value, back=False):
        place = jnp.arange(self.chips, dtype=jnp.int32)
        here = self.s // CORES & ~1
        if back:
            other = place ^ here
            return move_blocks(((other // 2 % 2) * self.hi + other // 4) * 2 + place % 2, value)
        hi, lo = place // 2 % self.hi, place // (2 * self.hi)
        return move_blocks((hi * 4 + lo * 2 + place % 2) ^ here, value)

    def gather_members(self, value, bits):
        for which in bits:
            value = jnp.concatenate([value, self.swap(value, which)], axis=0)
        return value

    def sum_members(self, partial, bits, wire=None):
        wire, total = wire or partial.dtype, partial
        for which in bits[::-1]:
            half = total.shape[0] // 2
            total = total[:half].astype(F32) + self.swap(total[half:].astype(wire), which).astype(F32)
        return total

    def join_his(self, value):
        for which in self.his:
            value = self.join(value, which)
        return value.reshape((self.hi,) + value.shape[len(self.his) :])

    def reduce_his(self, value):
        value = value.reshape((2,) * len(self.his) + value.shape[1:])
        for which in self.his[::-1]:
            value = self.reduce(value, which, 0)
        return value

    def join_reps(self, value):
        for which in self.rep_bits:
            value = self.join(value, which)
        return value.reshape((self.reps,) + value.shape[len(self.rep_bits) :])

    def own_rep(self, weight):
        return lax.dynamic_index_in_dim(weight.reshape(self.reps, -1, weight.shape[1]), self.r, 0, keepdims=False)

    def groups(self, bits):
        flips = [value * self.shards if axis == "rep" else value for axis, value in bits]
        group = [0]
        for flip in flips:
            group = group + [n + flip for n in group]
        group = sorted(group)
        return [[base + n for n in group] for base in range(self.reps * self.shards) if not base & sum(flips)]

    def gather_group(self, value):
        return lax.all_gather(value, AXES, axis=0, tiled=True, axis_index_groups=self.groups(self.feeders))

    def sum_group(self, value):
        return lax.psum_scatter(value, AXES, scatter_dimension=0, tiled=True, axis_index_groups=self.groups(self.feeders)).astype(F32)


def fence(*values):
    return lax.optimization_barrier(values)


def late(value, *others):
    return fence(value, *others)[0]


def chooser(sources, targets, source_of):
    row = lax.broadcasted_iota(jnp.int32, (sources, targets), 0)
    column = lax.broadcasted_iota(jnp.int32, (sources, targets), 1)
    return (row == source_of(column)).astype(BF16)


def shards(
    reps,
    places,
    tokens,
    segment_ids,
    norm_gain,
    input_weight,
    forget_weight,
    gate_weight,
    mixer_gain,
    out_weight,
    ffn_gain,
    ffn_gate_weight,
    ffn_up_weight,
    ffn_down_weight,
    cotangent,
):
    at = Place(reps, places)
    inputs = tokens[0].astype(F32)
    length, width = inputs.shape
    units = ffn_up_weight.shape[1]
    count = 2 ** len(at.mixers)
    channels = width // count
    part = units // 2 ** len(at.feeders)
    rows = width // places
    small = rows // reps
    slim = units // (places * reps)
    chip_rows = CORES * rows

    def channel_source(position):
        core, chip, inner = position // channels, position % channels // small, position % small
        return ((chip * CORES + core) * reps + at.r) * small + inner

    triple_rows = jnp.concatenate([input_weight, forget_weight, gate_weight])
    picked = matmul(triple_rows, chooser(width, CORES * channels, channel_source), (1, 0), BF16)
    picked = picked.reshape(3, rows, CORES, channels).transpose(1, 2, 0, 3).reshape(rows, -1)
    mix_all = lax.all_gather(picked, "shard", axis=0, tiled=True)

    pair_rows = jnp.concatenate([ffn_gate_weight, ffn_up_weight])

    def pick_units(core):
        def column(low):
            def source(position):
                line, inner = position // slim, position % slim
                return (((line * 2 + low) * CORES + core) * reps + at.r) * slim + inner

            return source

        return jnp.concatenate([matmul(pair_rows, chooser(units, part, column(low)), (1, 0), BF16) for low in range(2)])

    kept, given = pick_units(at.c), pick_units(1 - at.c)

    grad_out = cotangent[0]
    all_tokens = at.gather_members(tokens[0], at.mixers)
    segments = at.gather_members(segment_ids, at.mixers)
    starts = jnp.zeros((count, 1), F32)
    same = jnp.concatenate([starts, (segments[:, 1:] == segments[:, :-1]).astype(F32)], axis=1)
    same = same.reshape(count * length, 1)
    out_lines = at.join_his(at.own_rep(out_weight))
    out_lines, own_gains = fence(out_lines, jnp.stack([norm_gain, mixer_gain, ffn_gain]))
    out_rows = at.join(at.join(out_lines, at.lo, 1), at.low, 2).reshape(channels, width)
    gains = lax.all_gather(own_gains, "shard", axis=1, tiled=True).astype(F32)
    gain_one, gain_two, gain_three = gains[0], gains[1], gains[2]
    gain_grid = gain_two.reshape(at.chips, CORES, reps, small)
    gain_mix = lax.dynamic_index_in_dim(lax.dynamic_index_in_dim(gain_grid, at.c, 1, keepdims=False), at.r, 1, keepdims=False).reshape(-1)
    normed = (normalize(all_tokens.astype(F32))[0] * gain_one).astype(BF16)
    lines = lambda value: value.reshape(2 * CORES, rows, part)
    chip = at.merge(lines(kept), lines(at.swap(given, at.core)), at.core, 1).reshape(2, CORES * chip_rows, part)
    own_pair = at.trade(chip, at.low, 0)
    mix_all, normed, same, own_pair, out_rows, grad_out_sent, own_down = fence(
        mix_all, normed, same, own_pair, out_rows, grad_out, at.own_rep(ffn_down_weight)
    )

    all_grad_out = at.gather_group(grad_out_sent)
    pair_grid = own_pair.reshape(2, 2, chip_rows, part)
    gate_half, up_half = pair_grid[:, 0].reshape(-1, part), pair_grid[:, 1].reshape(-1, part)
    for which in at.his:
        gate_half = at.extend(gate_half, which)
    mix_weight = lax.dynamic_slice_in_dim(mix_all, at.c * (3 * channels), 3 * channels, 1)
    pre = matmul(normed, mix_weight, (1, 0))
    input_pre, forget_pre, gate_pre = (pre[:, k * channels : (k + 1) * channels] for k in range(3))
    forget = jax.nn.sigmoid(forget_pre)
    input_act, input_slope = swish_pair(input_pre)
    decay = forget * same
    state = run_scan(scan_forward_kernel, "scan_forward", count, length, decay, input_act * (1.0 - forget))
    gate_act, gate_slope = swish_pair(gate_pre)
    mixed_raw = (state * gain_mix * gate_act).astype(BF16)
    squares = jnp.sum(state * state, axis=1).reshape(count, length)
    out_part, squares, gate_half, up_half = fence(matmul(mixed_raw, out_rows, (1, 0), BF16), squares, gate_half, up_half)

    gate_columns = at.extend(gate_half, at.lo)
    for which in at.his:
        up_half = at.extend(up_half, which)
    square_sum = at.sum_members(squares, at.mixers)
    branch_sum = at.sum_members(out_part, at.mixers)
    branch_sum, square_sum, gate_columns, up_half, own_down = fence(branch_sum, square_sum, gate_columns, up_half, own_down)

    up_columns = at.extend(up_half, at.lo)
    down_lines = at.join_his(own_down)
    state_scale = lax.rsqrt(square_sum / width + EPSILON)
    branch = branch_sum * state_scale.reshape(length, 1)
    resid = inputs + branch
    scaled_mid, scale_mid = normalize(resid)
    ffn_in = at.gather_group(at.block_order((scaled_mid * gain_three).astype(BF16)))
    ffn_in, up_columns, down_lines, all_grad_out = fence(ffn_in, up_columns, down_lines, all_grad_out)
    down_rows = at.join(down_lines, at.lo, 1).reshape(part, width)
    ffn_gate = matmul(ffn_in, gate_columns, (1, 0))
    ffn_up = matmul(ffn_in, up_columns, (1, 0))
    ffn_act, ffn_slope = swish_pair(ffn_gate)
    hidden = (ffn_act * ffn_up).astype(BF16)
    down_cut = matmul(hidden, all_grad_out, (0, 0), BF16)
    down_rows, down_cut, hidden = fence(down_rows, down_cut, hidden)
    grad_hidden = matmul(all_grad_out, down_rows, (1, 1))
    grad_fgate = (grad_hidden * ffn_up * ffn_slope).astype(BF16)
    grad_fup = (grad_hidden * ffn_act).astype(BF16)
    grad_cut = (matmul(grad_fgate, gate_columns, (1, 1)) + matmul(grad_fup, up_columns, (1, 1))).astype(BF16)
    grad_cut, grad_fgate, grad_fup, down_cut = fence(grad_cut, grad_fgate, grad_fup, down_cut)

    grad_ffn_in = at.sum_group(grad_cut)
    down_line = at.reduce(down_cut.reshape(at.hi, 2, -1, width), at.lo, 1)
    gate_line = at.fold(matmul(ffn_in, grad_fgate, (0, 0), BF16), at.lo)
    up_cut = matmul(ffn_in, grad_fup, (0, 0), BF16)
    ffn_part = matmul(hidden, down_rows, (1, 0), BF16)
    down_line, ffn_part, up_cut = fence(down_line, ffn_part, up_cut)
    down_own = at.reduce_his(down_line)
    grad_ffn_in, gate_line, down_own, ffn_part, up_cut = fence(grad_ffn_in, gate_line, down_own, ffn_part, up_cut)

    def fold_begin(lines, which):
        half = lines.shape[0] // 2
        return (lines[:half], at.swap(lines[half:], which))

    def fold_rest(lines):
        for which in at.his[-2::-1]:
            lines = at.fold(lines, which)
        return lines

    mates = lambda lines: at.trade(lines.reshape(2, chip_rows, part), at.low, 0)
    cores = lambda sets: at.trade(sets.reshape(-1, CORES, rows, sets.shape[-1]), at.core, 1)
    up_line = at.fold(up_cut, at.lo)
    ffn_out = at.sum_group(ffn_part)
    grad_ffn_in = at.block_order(grad_ffn_in.astype(BF16), True).astype(F32)
    grad_resid = grad_out.astype(F32) + norm_back(grad_ffn_in * gain_three, scaled_mid, scale_mid)
    grad_branch_own = grad_resid.astype(BF16)
    inner_own = jnp.mean(grad_branch_own.astype(F32) * branch, axis=1)
    row_facts = at.gather_members(jnp.stack([state_scale.reshape(length), inner_own])[None], at.mixers)
    grad_branch = at.gather_members(grad_branch_own, at.mixers)
    grad_branch, row_facts, up_line, gate_line = fence(grad_branch, row_facts, up_line, gate_line)

    gate_hi = fold_rest(at.end(*fold_begin(gate_line, at.his[-1])))
    all_scale = row_facts[:, 0].reshape(count * length, 1)
    all_inner = row_facts[:, 1].reshape(count * length, 1)
    state_scaled = state * all_scale
    mixed = (state_scaled * gain_mix * gate_act).astype(BF16)
    weighted = matmul(grad_branch, out_rows, (1, 1)) * gain_mix
    plane = lambda cut: cut.reshape(at.hi, 2, 2, -1, cut.shape[1])
    out_keep, out_other = at.begin(plane(matmul(mixed, grad_branch, (0, 0), BF16)), at.low, 2)
    grad_gate_pre = (weighted * state_scaled * gate_slope).astype(BF16)
    grad_state = all_scale * (weighted * gate_act - state_scaled * all_inner)
    carried = run_scan(scan_backward_kernel, "scan_backward", count, length, decay, grad_state)
    line = state.reshape(count, length, channels)
    previous = jnp.concatenate([jnp.zeros((count, 1, channels), F32), line[:, :-1]], axis=1).reshape(state.shape)
    grad_forget = carried * previous * same - carried * input_act
    grad_input_pre = (carried * (1.0 - forget) * input_slope).astype(BF16)
    grad_forget_pre = (grad_forget * forget * (1.0 - forget)).astype(BF16)
    cut_a, cut_b, cut_c = (plane(matmul(normed, g, (0, 0), BF16)) for g in (grad_gate_pre, grad_input_pre, grad_forget_pre))
    out_keep, cut_a, cut_b, cut_c, up_line, gate_hi, ffn_out, down_own, grad_input_pre, grad_forget_pre = fence(
        out_keep, cut_a, cut_b, cut_c, up_line, gate_hi, ffn_out, down_own, grad_input_pre, grad_forget_pre
    )

    sum_low = lambda cut: at.reduce(cut, at.low, 2)
    sum_lo = lambda line: at.reduce(line, at.lo, 1)
    triple = jnp.concatenate([grad_input_pre, grad_forget_pre, grad_gate_pre], axis=1)
    normed_cut = matmul(triple, mix_weight, (1, 1), BF16)
    gate_sets, out_low = mates(gate_hi), at.end(out_keep, out_other)
    keep_a, other_a = at.begin(cut_a, at.low, 2)
    up_keep, up_other = fold_begin(up_line, at.his[-1])
    gate_sets, out_low, keep_a, cut_b, cut_c, up_keep, normed_cut, down_own = fence(
        gate_sets, out_low, keep_a, cut_b, cut_c, up_keep, normed_cut, down_own
    )
    keep_b, other_b = at.begin(cut_b, at.low, 2)
    normed_half = at.sum_members(normed_cut, [at.core])
    low_a, out_lo, gate_cores, up_hi = at.end(keep_a, other_a), sum_lo(out_low), cores(gate_sets), fold_rest(at.end(up_keep, up_other))
    low_a, out_lo, gate_cores, up_hi, keep_b, cut_c, normed_half, down_own = fence(
        low_a, out_lo, gate_cores, up_hi, keep_b, cut_c, normed_half, down_own
    )
    grad_normed = at.sum_members(normed_half, at.rep_bits, BF16)
    up_sets, gate_own = mates(up_hi), at.join_reps(gate_cores)
    keep_c, other_c = at.begin(cut_c, at.low, 2)
    low_b, lo_a, out_own = at.end(keep_b, other_b), sum_lo(low_a), at.reduce_his(out_lo)
    low_b, lo_a, out_own, keep_c, up_sets, down_own = fence(low_b, lo_a, out_own, keep_c, up_sets, down_own)
    down_own = at.join_reps(down_own)
    low_c, lo_b, hi_a, up_cores = at.end(keep_c, other_c), sum_lo(low_b), at.reduce_his(lo_a), cores(up_sets)
    low_c, lo_b, hi_a, up_cores = fence(low_c, lo_b, hi_a, up_cores)
    up_own, lo_c, hi_b, own_a = at.join_reps(up_cores), sum_lo(low_c), at.reduce_his(lo_b), cores(hi_a)
    lo_c, hi_b, own_a, out_own, gate_own, grad_normed = fence(lo_c, hi_b, own_a, out_own, gate_own, grad_normed)
    hi_c, own_b, own_a, out_own = at.reduce_his(lo_c), cores(hi_b), at.join_reps(own_a), at.join_reps(out_own)
    hi_c, own_b = fence(hi_c, own_b)
    own_c, own_b = cores(hi_c), at.join_reps(own_b)
    own_c, gate_own, up_own, out_own, down_own, grad_normed, ffn_out = fence(own_c, gate_own, up_own, out_own, down_own, grad_normed, ffn_out)
    mix_owns = [own_b, at.join_reps(own_c), own_a]
    block_output = (resid + ffn_out).astype(BF16)
    scaled_in, scale_in = normalize(inputs)
    input_grad = (grad_resid + norm_back(grad_normed * gain_one, scaled_in, scale_in)).astype(BF16)

    def channel_place(column):
        chip, core = column // (CORES * reps * small), column // (reps * small) % CORES
        return ((column // small % reps * CORES + core) * at.chips + chip) * small + column % small

    def whole_channels(owns):
        lines = jnp.stack(owns).reshape(len(owns), reps * CORES, rows, channels).transpose(0, 2, 1, 3).reshape(-1, width)
        return jnp.split(matmul(lines, chooser(width, width, channel_place), (1, 0)), len(owns))

    def whole_units(own):
        grid = own.reshape(reps, CORES, 2, rows, at.length, slim)
        return grid.transpose(3, 4, 2, 1, 0, 5).reshape(rows, units).astype(F32)

    def whole_rows(own):
        return own.reshape(-1, width).astype(F32)

    down_total = whole_rows(down_own)
    gate_total, up_total = whole_units(gate_own), whole_units(up_own)
    out_total = whole_rows(out_own)
    mix_totals = whole_channels(mix_owns)
    dotted = lambda w, g: jnp.sum(w.astype(F32) * g, axis=1)
    norm_gain_grad = sum(dotted(w, g) for w, g in zip((input_weight, forget_weight, gate_weight), mix_totals)) / norm_gain.astype(F32)
    mixer_gain_grad = dotted(out_weight, out_total) / mixer_gain.astype(F32)
    ffn_gain_grad = (dotted(ffn_gate_weight, gate_total) + dotted(ffn_up_weight, up_total)) / ffn_gain.astype(F32)
    return (
        block_output[None],
        input_grad[None],
        norm_gain_grad,
        *mix_totals,
        mixer_gain_grad,
        out_total,
        ffn_gain_grad,
        gate_total,
        up_total,
        down_total,
    )


def solution(mesh):
    tokens, vector, matrix = P(AXES, None, None), P("shard"), P("shard", None)
    placed = (tokens, P(AXES, None), vector, matrix, matrix, matrix, vector, matrix, vector, matrix, matrix, matrix, tokens)
    return jax.shard_map(
        functools.partial(shards, mesh.shape["rep"], mesh.shape["shard"]),
        mesh=mesh,
        in_specs=placed,
        out_specs=(tokens, tokens, vector, matrix, matrix, matrix, vector, matrix, vector, matrix, matrix, matrix),
        check_vma=False,
    )
```

```python
import functools

import jax
import jax.numpy as jnp
from jax import lax
from jax.experimental import pallas as pl
from jax.experimental.pallas import tpu as pltpu
from jax.sharding import PartitionSpec as P

EPSILON = 1e-06
AXES = ("rep", "shard")
CORES = 2
F32 = jnp.float32
BF16 = jnp.bfloat16


def normalize(values):
    scale = lax.rsqrt(jnp.mean(values * values, axis=-1, keepdims=True) + EPSILON)
    return (values * scale, scale)


def norm_back(grad_scaled, scaled, scale):
    inner = jnp.mean(grad_scaled * scaled, axis=-1, keepdims=True)
    return scale * (grad_scaled - scaled * inner)


def swish_pair(values):
    sigma = jax.nn.sigmoid(values)
    return (values * sigma, sigma * (1.0 + values * (1.0 - sigma)))


def matmul(left, right, dims, out=F32):
    return lax.dot_general(left, right, ((dims[:1], dims[1:]), ((), ())), preferred_element_type=F32).astype(out)


TILE = 8


def scan_tile(decay, update, reverse):
    row = lax.broadcasted_iota(jnp.int32, decay.shape, 0)
    for step in (1, 2, 4):
        shift = TILE - step if reverse else step
        inside = row < TILE - step if reverse else row >= step
        earlier = jnp.where(inside, pltpu.roll(update, shift, 0), 0.0)
        product = jnp.where(inside, pltpu.roll(decay, shift, 0), 1.0)
        update = update + decay * earlier
        decay = decay * product
    return (decay, update)


def scan_forward_kernel(count, length, decay, update, state):
    def block(step, carries):
        out = []
        for n in range(count):
            rows = pl.ds(pl.multiple_of(n * length + step * TILE, TILE), TILE)
            product, local = scan_tile(decay[rows, :], update[rows, :], False)
            local = local + product * carries[n]
            state[rows, :] = local
            out.append(local[TILE - 1 :, :])
        return tuple(out)

    lax.fori_loop(0, length // TILE, block, (jnp.zeros((1, state.shape[1]), F32),) * count)


def scan_backward_kernel(count, length, decay, grad, carried):
    steps = length // TILE

    def block(step, pairs):
        out = []
        for n in range(count):
            carry, later = pairs[n]
            rows = pl.ds(pl.multiple_of(n * length + (steps - 1 - step) * TILE, TILE), TILE)
            own = decay[rows, :]
            row = lax.broadcasted_iota(jnp.int32, own.shape, 0)
            following = jnp.where(row < TILE - 1, pltpu.roll(own, TILE - 1, 0), later)
            product, local = scan_tile(following, grad[rows, :], True)
            local = local + product * carry
            carried[rows, :] = local
            out.append((local[:1, :], own[:1, :]))
        return tuple(out)

    zero = jnp.zeros((1, carried.shape[1]), F32)
    lax.fori_loop(0, steps, block, ((zero, zero),) * count)


def run_scan(kernel, name, count, length, left, right):
    size = left.size
    return pl.pallas_call(
        functools.partial(kernel, count, length),
        out_shape=jax.ShapeDtypeStruct(left.shape, F32),
        in_specs=[pl.BlockSpec(memory_space=pltpu.VMEM)] * 2,
        out_specs=pl.BlockSpec(memory_space=pltpu.VMEM),
        compiler_params=pltpu.CompilerParams(vmem_limit_bytes=32 * 2**20),
        cost_estimate=pl.CostEstimate(flops=2 * size, bytes_accessed=12 * size, transcendentals=0),
        name=name,
    )(left, right)


def move_kernel(blocks, source, value, out):
    wide = value.shape[1] // blocks
    for k in range(blocks):
        out[:, k * wide : (k + 1) * wide] = value[:, pl.ds(pl.multiple_of(source[k] * wide, 128), wide)]


def move_blocks(source, value):
    return pl.pallas_call(
        functools.partial(move_kernel, source.shape[0]),
        out_shape=jax.ShapeDtypeStruct(value.shape, value.dtype),
        in_specs=[pl.BlockSpec(memory_space=pltpu.SMEM), pl.BlockSpec(memory_space=pltpu.VMEM)],
        out_specs=pl.BlockSpec(memory_space=pltpu.VMEM),
        cost_estimate=pl.CostEstimate(flops=0, bytes_accessed=2 * value.size * value.dtype.itemsize, transcendentals=0),
        name="move_blocks",
    )(source, value)


class Place:
    def __init__(self, reps, shards):
        self.reps, self.shards = reps, shards
        self.chips = shards // CORES
        self.hi = self.chips // 4
        self.length = self.chips // 2
        self.r = lax.axis_index("rep")
        self.s = lax.axis_index("shard")
        self.c = self.s % CORES
        self.core = ("shard", 1)
        self.low = ("shard", 2)
        self.lo = ("shard", 4)
        self.his = [("shard", 8 << k) for k in range(self.hi.bit_length() - 1)]
        self.rep_bits = [("rep", 1 << k) for k in range(reps.bit_length() - 1)]
        self.mixers = self.rep_bits + [self.core]
        self.feeders = self.rep_bits + [self.low, self.core]

    def bit(self, which):
        axis, value = which
        return ((self.r if axis == "rep" else self.s) // value) % 2

    def swap(self, value, which):
        axis, flip = which
        flip = flip * self.shards if axis == "rep" else flip
        return lax.ppermute(value, AXES, [(n, n ^ flip) for n in range(self.reps * self.shards)])

    def merge(self, own, other, which, axis=0):
        first = self.bit(which) == 0
        return jnp.stack([jnp.where(first, own, other), jnp.where(first, other, own)], axis)

    def join(self, value, which, axis=0):
        return self.merge(value, self.swap(value, which), which, axis)

    def pick(self, value, which, axis, flipped=False):
        bit = self.bit(which)
        return lax.dynamic_index_in_dim(value, 1 - bit if flipped else bit, axis, keepdims=False)

    def trade(self, value, which, axis):
        other = self.swap(self.pick(value, which, axis, True), which)
        return self.merge(self.pick(value, which, axis), other, which)

    def reduce(self, value, which, axis):
        other = self.swap(self.pick(value, which, axis, True), which)
        return (self.pick(value, which, axis).astype(F32) + other.astype(F32)).astype(BF16)

    def begin(self, value, which, axis):
        return (self.pick(value, which, axis), self.swap(self.pick(value, which, axis, True), which))

    def end(self, own, other):
        return (own.astype(F32) + other.astype(F32)).astype(BF16)

    def extend(self, value, which):
        return jnp.concatenate([value, self.swap(value, which)], axis=0)

    def fold(self, value, which):
        half = value.shape[0] // 2
        other = self.swap(value[half:], which)
        return (value[:half].astype(F32) + other.astype(F32)).astype(BF16)

    def block_order(self, value, back=False):
        place = jnp.arange(self.chips, dtype=jnp.int32)
        here = self.s // CORES & ~1
        if back:
            other = place ^ here
            return move_blocks(((other // 2 % 2) * self.hi + other // 4) * 2 + place % 2, value)
        hi, lo = place // 2 % self.hi, place // (2 * self.hi)
        return move_blocks((hi * 4 + lo * 2 + place % 2) ^ here, value)

    def gather_members(self, value, bits):
        for which in bits:
            value = jnp.concatenate([value, self.swap(value, which)], axis=0)
        return value

    def sum_members(self, partial, bits, wire=None):
        wire, total = wire or partial.dtype, partial
        for which in bits[::-1]:
            half = total.shape[0] // 2
            total = total[:half].astype(F32) + self.swap(total[half:].astype(wire), which).astype(F32)
        return total

    def join_his(self, value):
        for which in self.his:
            value = self.join(value, which)
        return value.reshape((self.hi,) + value.shape[len(self.his) :])

    def reduce_his(self, value):
        value = value.reshape((2,) * len(self.his) + value.shape[1:])
        for which in self.his[::-1]:
            value = self.reduce(value, which, 0)
        return value

    def join_reps(self, value):
        for which in self.rep_bits:
            value = self.join(value, which)
        return value.reshape((self.reps,) + value.shape[len(self.rep_bits) :])

    def own_rep(self, weight):
        return lax.dynamic_index_in_dim(weight.reshape(self.reps, -1, weight.shape[1]), self.r, 0, keepdims=False)

    def groups(self, bits):
        flips = [value * self.shards if axis == "rep" else value for axis, value in bits]
        group = [0]
        for flip in flips:
            group = group + [n + flip for n in group]
        group = sorted(group)
        return [[base + n for n in group] for base in range(self.reps * self.shards) if not base & sum(flips)]

    def gather_group(self, value):
        return lax.all_gather(value, AXES, axis=0, tiled=True, axis_index_groups=self.groups(self.feeders))

    def sum_group(self, value):
        return lax.psum_scatter(value, AXES, scatter_dimension=0, tiled=True, axis_index_groups=self.groups(self.feeders)).astype(F32)


def fence(*values):
    return lax.optimization_barrier(values)


def late(value, *others):
    return fence(value, *others)[0]


def chooser(sources, targets, source_of):
    row = lax.broadcasted_iota(jnp.int32, (sources, targets), 0)
    column = lax.broadcasted_iota(jnp.int32, (sources, targets), 1)
    return (row == source_of(column)).astype(BF16)


def shards(
    reps,
    places,
    tokens,
    segment_ids,
    norm_gain,
    input_weight,
    forget_weight,
    gate_weight,
    mixer_gain,
    out_weight,
    ffn_gain,
    ffn_gate_weight,
    ffn_up_weight,
    ffn_down_weight,
    cotangent,
):
    at = Place(reps, places)
    inputs = tokens[0].astype(F32)
    length, width = inputs.shape
    units = ffn_up_weight.shape[1]
    count = 2 ** len(at.mixers)
    channels = width // count
    part = units // 2 ** len(at.feeders)
    rows = width // places
    small = rows // reps
    slim = units // (places * reps)
    chip_rows = CORES * rows

    def channel_source(position):
        core, chip, inner = position // channels, position % channels // small, position % small
        return ((chip * CORES + core) * reps + at.r) * small + inner

    triple_rows = jnp.concatenate([input_weight, forget_weight, gate_weight])
    picked = matmul(triple_rows, chooser(width, CORES * channels, channel_source), (1, 0), BF16)
    picked = picked.reshape(3, rows, CORES, channels).transpose(1, 2, 0, 3).reshape(rows, -1)
    mix_all = lax.all_gather(picked, "shard", axis=0, tiled=True)

    pair_rows = jnp.concatenate([ffn_gate_weight, ffn_up_weight])

    def pick_units(core):
        def column(low):
            def source(position):
                line, inner = position // slim, position % slim
                return (((line * 2 + low) * CORES + core) * reps + at.r) * slim + inner

            return source

        return jnp.concatenate([matmul(pair_rows, chooser(units, part, column(low)), (1, 0), BF16) for low in range(2)])

    kept, given = pick_units(at.c), pick_units(1 - at.c)

    grad_out = cotangent[0]
    all_tokens = at.gather_members(tokens[0], at.mixers)
    segments = at.gather_members(segment_ids, at.mixers)
    starts = jnp.zeros((count, 1), F32)
    same = jnp.concatenate([starts, (segments[:, 1:] == segments[:, :-1]).astype(F32)], axis=1)
    same = same.reshape(count * length, 1)
    out_lines = at.join_his(at.own_rep(out_weight))
    out_lines, own_gains = fence(out_lines, jnp.stack([norm_gain, mixer_gain, ffn_gain]))
    out_rows = at.join(at.join(out_lines, at.lo, 1), at.low, 2).reshape(channels, width)
    gains = lax.all_gather(own_gains, "shard", axis=1, tiled=True).astype(F32)
    gain_one, gain_two, gain_three = gains[0], gains[1], gains[2]
    gain_grid = gain_two.reshape(at.chips, CORES, reps, small)
    gain_mix = lax.dynamic_index_in_dim(lax.dynamic_index_in_dim(gain_grid, at.c, 1, keepdims=False), at.r, 1, keepdims=False).reshape(-1)
    normed = (normalize(all_tokens.astype(F32))[0] * gain_one).astype(BF16)
    lines = lambda value: value.reshape(2 * CORES, rows, part)
    chip = at.merge(lines(kept), lines(at.swap(given, at.core)), at.core, 1).reshape(2, CORES * chip_rows, part)
    own_pair = at.trade(chip, at.low, 0)
    pair_grid = own_pair.reshape(2, 2, chip_rows, part)
    gate_half, up_half = pair_grid[:, 0].reshape(-1, part), pair_grid[:, 1].reshape(-1, part)
    mix_all, normed, same, gate_half, up_half, out_rows, grad_out_sent, own_down = fence(
        mix_all, normed, same, gate_half, up_half, out_rows, grad_out, at.own_rep(ffn_down_weight)
    )

    all_grad_out = at.gather_group(grad_out_sent)
    for which in at.his:
        gate_half = at.extend(gate_half, which)
    mix_weight = lax.dynamic_slice_in_dim(mix_all, at.c * (3 * channels), 3 * channels, 1)
    pre = matmul(normed, mix_weight, (1, 0))
    input_pre, forget_pre, gate_pre = (pre[:, k * channels : (k + 1) * channels] for k in range(3))
    forget = jax.nn.sigmoid(forget_pre)
    input_act, input_slope = swish_pair(input_pre)
    decay = forget * same
    state = run_scan(scan_forward_kernel, "scan_forward", count, length, decay, input_act * (1.0 - forget))
    gate_act, gate_slope = swish_pair(gate_pre)
    mixed_raw = (state * gain_mix * gate_act).astype(BF16)
    squares = jnp.sum(state * state, axis=1).reshape(count, length)
    out_part, squares, gate_half, up_half = fence(matmul(mixed_raw, out_rows, (1, 0), BF16), squares, gate_half, up_half)

    gate_columns = at.extend(gate_half, at.lo)
    for which in at.his:
        up_half = at.extend(up_half, which)
    square_sum = at.sum_members(squares, at.mixers)
    branch_sum = at.sum_members(out_part, at.mixers)
    branch_sum, square_sum, gate_columns, up_half, own_down = fence(branch_sum, square_sum, gate_columns, up_half, own_down)

    up_columns = at.extend(up_half, at.lo)
    down_lines = at.join_his(own_down)
    state_scale = lax.rsqrt(square_sum / width + EPSILON)
    branch = branch_sum * state_scale.reshape(length, 1)
    resid = inputs + branch
    scaled_mid, scale_mid = normalize(resid)
    ffn_in = at.gather_group(at.block_order((scaled_mid * gain_three).astype(BF16)))
    ffn_in, up_columns, down_lines, all_grad_out = fence(ffn_in, up_columns, down_lines, all_grad_out)
    down_rows = at.join(down_lines, at.lo, 1).reshape(part, width)
    ffn_gate = matmul(ffn_in, gate_columns, (1, 0))
    ffn_up = matmul(ffn_in, up_columns, (1, 0))
    ffn_act, ffn_slope = swish_pair(ffn_gate)
    hidden = (ffn_act * ffn_up).astype(BF16)
    down_cut = matmul(hidden, all_grad_out, (0, 0), BF16)
    down_rows, down_cut, hidden = fence(down_rows, down_cut, hidden)
    grad_hidden = matmul(all_grad_out, down_rows, (1, 1))
    grad_fgate = (grad_hidden * ffn_up * ffn_slope).astype(BF16)
    grad_fup = (grad_hidden * ffn_act).astype(BF16)
    grad_cut = (matmul(grad_fgate, gate_columns, (1, 1)) + matmul(grad_fup, up_columns, (1, 1))).astype(BF16)
    grad_cut, grad_fgate, grad_fup, down_cut = fence(grad_cut, grad_fgate, grad_fup, down_cut)

    grad_ffn_in = at.sum_group(grad_cut)
    down_line = at.reduce(down_cut.reshape(at.hi, 2, -1, width), at.lo, 1)
    gate_line = at.fold(matmul(ffn_in, grad_fgate, (0, 0), BF16), at.lo)
    up_cut = matmul(ffn_in, grad_fup, (0, 0), BF16)
    ffn_part = matmul(hidden, down_rows, (1, 0), BF16)
    down_line, ffn_part, up_cut = fence(down_line, ffn_part, up_cut)
    down_own = at.reduce_his(down_line)
    grad_ffn_in, gate_line, down_own, ffn_part, up_cut = fence(grad_ffn_in, gate_line, down_own, ffn_part, up_cut)

    def fold_begin(lines, which):
        half = lines.shape[0] // 2
        return (lines[:half], at.swap(lines[half:], which))

    def fold_rest(lines):
        for which in at.his[-2::-1]:
            lines = at.fold(lines, which)
        return lines

    mates = lambda lines: at.trade(lines.reshape(2, chip_rows, part), at.low, 0)
    cores = lambda sets: at.trade(sets.reshape(-1, CORES, rows, sets.shape[-1]), at.core, 1)
    up_line = at.fold(up_cut, at.lo)
    ffn_out = at.sum_group(ffn_part)
    grad_ffn_in = at.block_order(grad_ffn_in.astype(BF16), True).astype(F32)
    grad_resid = grad_out.astype(F32) + norm_back(grad_ffn_in * gain_three, scaled_mid, scale_mid)
    grad_branch_own = grad_resid.astype(BF16)
    inner_own = jnp.mean(grad_branch_own.astype(F32) * branch, axis=1)
    row_facts = at.gather_members(jnp.stack([state_scale.reshape(length), inner_own])[None], at.mixers)
    grad_branch = at.gather_members(grad_branch_own, at.mixers)
    grad_branch, row_facts, up_line, gate_line, down_own = fence(grad_branch, row_facts, up_line, gate_line, down_own)

    down_own = at.join_reps(down_own)
    gate_hi = fold_rest(at.end(*fold_begin(gate_line, at.his[-1])))
    all_scale = row_facts[:, 0].reshape(count * length, 1)
    all_inner = row_facts[:, 1].reshape(count * length, 1)
    state_scaled = state * all_scale
    mixed = (state_scaled * gain_mix * gate_act).astype(BF16)
    weighted = matmul(grad_branch, out_rows, (1, 1)) * gain_mix
    plane = lambda cut: cut.reshape(at.hi, 2, 2, -1, cut.shape[1])
    out_keep, out_other = at.begin(plane(matmul(mixed, grad_branch, (0, 0), BF16)), at.low, 2)
    grad_gate_pre = (weighted * state_scaled * gate_slope).astype(BF16)
    grad_state = all_scale * (weighted * gate_act - state_scaled * all_inner)
    carried = run_scan(scan_backward_kernel, "scan_backward", count, length, decay, grad_state)
    line = state.reshape(count, length, channels)
    previous = jnp.concatenate([jnp.zeros((count, 1, channels), F32), line[:, :-1]], axis=1).reshape(state.shape)
    grad_forget = carried * previous * same - carried * input_act
    grad_input_pre = (carried * (1.0 - forget) * input_slope).astype(BF16)
    grad_forget_pre = (grad_forget * forget * (1.0 - forget)).astype(BF16)
    cut_a, cut_b, cut_c = (plane(matmul(normed, g, (0, 0), BF16)) for g in (grad_gate_pre, grad_input_pre, grad_forget_pre))
    triple = jnp.concatenate([grad_input_pre, grad_forget_pre, grad_gate_pre], axis=1)
    normed_cut = matmul(triple, mix_weight, (1, 1), BF16)
    out_keep, cut_a, cut_b, cut_c, up_line, gate_hi, ffn_out, down_own, normed_cut = fence(
        out_keep, cut_a, cut_b, cut_c, up_line, gate_hi, ffn_out, down_own, normed_cut
    )

    sum_low = lambda cut: at.reduce(cut, at.low, 2)
    sum_lo = lambda line: at.reduce(line, at.lo, 1)
    gate_sets, out_low = mates(gate_hi), at.end(out_keep, out_other)
    keep_a, other_a = at.begin(cut_a, at.low, 2)
    gate_sets, out_low, keep_a, cut_b, cut_c, up_line, normed_cut, down_own = fence(
        gate_sets, out_low, keep_a, cut_b, cut_c, up_line, normed_cut, down_own
    )
    up_keep, up_other = fold_begin(up_line, at.his[-1])
    keep_b, other_b = at.begin(cut_b, at.low, 2)
    normed_half = at.sum_members(normed_cut, [at.core])
    low_a, out_lo, gate_cores = at.end(keep_a, other_a), sum_lo(out_low), cores(gate_sets)
    low_a, out_lo, gate_cores, up_keep, keep_b, cut_c, normed_half, down_own = fence(
        low_a, out_lo, gate_cores, up_keep, keep_b, cut_c, normed_half, down_own
    )
    up_hi = fold_rest(at.end(up_keep, up_other))
    grad_normed = at.sum_members(normed_half, at.rep_bits, BF16)
    up_sets = mates(up_hi)
    keep_c, other_c = at.begin(cut_c, at.low, 2)
    low_b, lo_a, out_own = at.end(keep_b, other_b), sum_lo(low_a), at.reduce_his(out_lo)
    low_b, lo_a, out_own, keep_c, up_sets, gate_cores = fence(low_b, lo_a, out_own, keep_c, up_sets, gate_cores)
    gate_own = at.join_reps(gate_cores)
    low_c, lo_b, hi_a, up_cores = at.end(keep_c, other_c), sum_lo(low_b), at.reduce_his(lo_a), cores(up_sets)
    low_c, lo_b, hi_a, up_cores, grad_normed = fence(low_c, lo_b, hi_a, up_cores, grad_normed)
    up_own, lo_c, hi_b, own_a = at.join_reps(up_cores), sum_lo(low_c), at.reduce_his(lo_b), cores(hi_a)
    lo_c, hi_b, own_a, out_own, gate_own = fence(lo_c, hi_b, own_a, out_own, gate_own)
    hi_c, own_b, own_a, out_own = at.reduce_his(lo_c), cores(hi_b), at.join_reps(own_a), at.join_reps(out_own)
    hi_c, own_b = fence(hi_c, own_b)
    own_c, own_b = cores(hi_c), at.join_reps(own_b)
    own_c, gate_own, up_own, out_own, down_own, grad_normed, ffn_out = fence(own_c, gate_own, up_own, out_own, down_own, grad_normed, ffn_out)
    mix_owns = [own_b, at.join_reps(own_c), own_a]
    block_output = (resid + ffn_out).astype(BF16)
    scaled_in, scale_in = normalize(inputs)
    input_grad = (grad_resid + norm_back(grad_normed * gain_one, scaled_in, scale_in)).astype(BF16)

    def channel_place(column):
        chip, core = column // (CORES * reps * small), column // (reps * small) % CORES
        return ((column // small % reps * CORES + core) * at.chips + chip) * small + column % small

    def whole_channels(owns):
        lines = jnp.stack(owns).reshape(len(owns), reps * CORES, rows, channels).transpose(0, 2, 1, 3).reshape(-1, width)
        return jnp.split(matmul(lines, chooser(width, width, channel_place), (1, 0)), len(owns))

    def whole_units(own):
        grid = own.reshape(reps, CORES, 2, rows, at.length, slim)
        return grid.transpose(3, 4, 2, 1, 0, 5).reshape(rows, units).astype(F32)

    def whole_rows(own):
        return own.reshape(-1, width).astype(F32)

    down_total = whole_rows(down_own)
    gate_total, up_total = whole_units(gate_own), whole_units(up_own)
    out_total = whole_rows(out_own)
    mix_totals = whole_channels(mix_owns)
    dotted = lambda w, g: jnp.sum(w.astype(F32) * g, axis=1)
    norm_gain_grad = sum(dotted(w, g) for w, g in zip((input_weight, forget_weight, gate_weight), mix_totals)) / norm_gain.astype(F32)
    mixer_gain_grad = dotted(out_weight, out_total) / mixer_gain.astype(F32)
    ffn_gain_grad = (dotted(ffn_gate_weight, gate_total) + dotted(ffn_up_weight, up_total)) / ffn_gain.astype(F32)
    return (
        block_output[None],
        input_grad[None],
        norm_gain_grad,
        *mix_totals,
        mixer_gain_grad,
        out_total,
        ffn_gain_grad,
        gate_total,
        up_total,
        down_total,
    )


def solution(mesh):
    tokens, vector, matrix = P(AXES, None, None), P("shard"), P("shard", None)
    placed = (tokens, P(AXES, None), vector, matrix, matrix, matrix, vector, matrix, vector, matrix, matrix, matrix, tokens)
    return jax.shard_map(
        functools.partial(shards, mesh.shape["rep"], mesh.shape["shard"]),
        mesh=mesh,
        in_specs=placed,
        out_specs=(tokens, tokens, vector, matrix, matrix, matrix, vector, matrix, vector, matrix, matrix, matrix),
        check_vma=False,
    )
```

```python
import functools

import jax
import jax.numpy as jnp
from jax import lax
from jax.experimental import pallas as pl
from jax.experimental.pallas import tpu as pltpu
from jax.sharding import PartitionSpec as P

EPSILON = 1e-06
AXES = ("rep", "shard")
CORES = 2
F32 = jnp.float32
BF16 = jnp.bfloat16


def normalize(values):
    scale = lax.rsqrt(jnp.mean(values * values, axis=-1, keepdims=True) + EPSILON)
    return (values * scale, scale)


def norm_back(grad_scaled, scaled, scale):
    inner = jnp.mean(grad_scaled * scaled, axis=-1, keepdims=True)
    return scale * (grad_scaled - scaled * inner)


def swish_pair(values):
    sigma = jax.nn.sigmoid(values)
    return (values * sigma, sigma * (1.0 + values * (1.0 - sigma)))


def matmul(left, right, dims, out=F32):
    return lax.dot_general(left, right, ((dims[:1], dims[1:]), ((), ())), preferred_element_type=F32).astype(out)


TILE = 8


def scan_tile(decay, update, reverse):
    row = lax.broadcasted_iota(jnp.int32, decay.shape, 0)
    for step in (1, 2, 4):
        shift = TILE - step if reverse else step
        inside = row < TILE - step if reverse else row >= step
        earlier = jnp.where(inside, pltpu.roll(update, shift, 0), 0.0)
        product = jnp.where(inside, pltpu.roll(decay, shift, 0), 1.0)
        update = update + decay * earlier
        decay = decay * product
    return (decay, update)


def scan_forward_kernel(count, length, decay, update, state):
    def block(step, carries):
        out = []
        for n in range(count):
            rows = pl.ds(pl.multiple_of(n * length + step * TILE, TILE), TILE)
            product, local = scan_tile(decay[rows, :], update[rows, :], False)
            local = local + product * carries[n]
            state[rows, :] = local
            out.append(local[TILE - 1 :, :])
        return tuple(out)

    lax.fori_loop(0, length // TILE, block, (jnp.zeros((1, state.shape[1]), F32),) * count)


def scan_backward_kernel(count, length, decay, grad, carried):
    steps = length // TILE

    def block(step, pairs):
        out = []
        for n in range(count):
            carry, later = pairs[n]
            rows = pl.ds(pl.multiple_of(n * length + (steps - 1 - step) * TILE, TILE), TILE)
            own = decay[rows, :]
            row = lax.broadcasted_iota(jnp.int32, own.shape, 0)
            following = jnp.where(row < TILE - 1, pltpu.roll(own, TILE - 1, 0), later)
            product, local = scan_tile(following, grad[rows, :], True)
            local = local + product * carry
            carried[rows, :] = local
            out.append((local[:1, :], own[:1, :]))
        return tuple(out)

    zero = jnp.zeros((1, carried.shape[1]), F32)
    lax.fori_loop(0, steps, block, ((zero, zero),) * count)


def run_scan(kernel, name, count, length, left, right):
    size = left.size
    return pl.pallas_call(
        functools.partial(kernel, count, length),
        out_shape=jax.ShapeDtypeStruct(left.shape, F32),
        in_specs=[pl.BlockSpec(memory_space=pltpu.VMEM)] * 2,
        out_specs=pl.BlockSpec(memory_space=pltpu.VMEM),
        compiler_params=pltpu.CompilerParams(vmem_limit_bytes=32 * 2**20),
        cost_estimate=pl.CostEstimate(flops=2 * size, bytes_accessed=12 * size, transcendentals=0),
        name=name,
    )(left, right)


def move_kernel(blocks, source, value, out):
    wide = value.shape[1] // blocks
    for k in range(blocks):
        out[:, k * wide : (k + 1) * wide] = value[:, pl.ds(pl.multiple_of(source[k] * wide, 128), wide)]


def move_blocks(source, value):
    return pl.pallas_call(
        functools.partial(move_kernel, source.shape[0]),
        out_shape=jax.ShapeDtypeStruct(value.shape, value.dtype),
        in_specs=[pl.BlockSpec(memory_space=pltpu.SMEM), pl.BlockSpec(memory_space=pltpu.VMEM)],
        out_specs=pl.BlockSpec(memory_space=pltpu.VMEM),
        cost_estimate=pl.CostEstimate(flops=0, bytes_accessed=2 * value.size * value.dtype.itemsize, transcendentals=0),
        name="move_blocks",
    )(source, value)


class Place:
    def __init__(self, reps, shards):
        self.reps, self.shards = reps, shards
        self.chips = shards // CORES
        self.hi = self.chips // 4
        self.length = self.chips // 2
        self.r = lax.axis_index("rep")
        self.s = lax.axis_index("shard")
        self.c = self.s % CORES
        self.core = ("shard", 1)
        self.low = ("shard", 2)
        self.lo = ("shard", 4)
        self.his = [("shard", 8 << k) for k in range(self.hi.bit_length() - 1)]
        self.rep_bits = [("rep", 1 << k) for k in range(reps.bit_length() - 1)]
        self.mixers = self.rep_bits + [self.core]
        self.feeders = self.rep_bits + [self.low, self.core]

    def bit(self, which):
        axis, value = which
        return ((self.r if axis == "rep" else self.s) // value) % 2

    def swap(self, value, which):
        axis, flip = which
        flip = flip * self.shards if axis == "rep" else flip
        return lax.ppermute(value, AXES, [(n, n ^ flip) for n in range(self.reps * self.shards)])

    def merge(self, own, other, which, axis=0):
        first = self.bit(which) == 0
        return jnp.stack([jnp.where(first, own, other), jnp.where(first, other, own)], axis)

    def join(self, value, which, axis=0):
        return self.merge(value, self.swap(value, which), which, axis)

    def pick(self, value, which, axis, flipped=False):
        bit = self.bit(which)
        return lax.dynamic_index_in_dim(value, 1 - bit if flipped else bit, axis, keepdims=False)

    def trade(self, value, which, axis):
        other = self.swap(self.pick(value, which, axis, True), which)
        return self.merge(self.pick(value, which, axis), other, which)

    def reduce(self, value, which, axis):
        other = self.swap(self.pick(value, which, axis, True), which)
        return (self.pick(value, which, axis).astype(F32) + other.astype(F32)).astype(BF16)

    def begin(self, value, which, axis):
        return (self.pick(value, which, axis), self.swap(self.pick(value, which, axis, True), which))

    def end(self, own, other):
        return (own.astype(F32) + other.astype(F32)).astype(BF16)

    def extend(self, value, which):
        return jnp.concatenate([value, self.swap(value, which)], axis=0)

    def fold(self, value, which):
        half = value.shape[0] // 2
        other = self.swap(value[half:], which)
        return (value[:half].astype(F32) + other.astype(F32)).astype(BF16)

    def block_order(self, value, back=False):
        place = jnp.arange(self.chips, dtype=jnp.int32)
        here = self.s // CORES & ~1
        if back:
            other = place ^ here
            return move_blocks(((other // 2 % 2) * self.hi + other // 4) * 2 + place % 2, value)
        hi, lo = place // 2 % self.hi, place // (2 * self.hi)
        return move_blocks((hi * 4 + lo * 2 + place % 2) ^ here, value)

    def gather_members(self, value, bits):
        for which in bits:
            value = jnp.concatenate([value, self.swap(value, which)], axis=0)
        return value

    def sum_members(self, partial, bits, wire=None):
        wire, total = wire or partial.dtype, partial
        for which in bits[::-1]:
            half = total.shape[0] // 2
            total = total[:half].astype(F32) + self.swap(total[half:].astype(wire), which).astype(F32)
        return total

    def join_his(self, value):
        for which in self.his:
            value = self.join(value, which)
        return value.reshape((self.hi,) + value.shape[len(self.his) :])

    def reduce_his(self, value):
        value = value.reshape((2,) * len(self.his) + value.shape[1:])
        for which in self.his[::-1]:
            value = self.reduce(value, which, 0)
        return value

    def join_reps(self, value):
        for which in self.rep_bits:
            value = self.join(value, which)
        return value.reshape((self.reps,) + value.shape[len(self.rep_bits) :])

    def own_rep(self, weight):
        return lax.dynamic_index_in_dim(weight.reshape(self.reps, -1, weight.shape[1]), self.r, 0, keepdims=False)

    def groups(self, bits):
        flips = [value * self.shards if axis == "rep" else value for axis, value in bits]
        group = [0]
        for flip in flips:
            group = group + [n + flip for n in group]
        group = sorted(group)
        return [[base + n for n in group] for base in range(self.reps * self.shards) if not base & sum(flips)]

    def gather_group(self, value):
        return lax.all_gather(value, AXES, axis=0, tiled=True, axis_index_groups=self.groups(self.feeders))

    def sum_group(self, value):
        return lax.psum_scatter(value, AXES, scatter_dimension=0, tiled=True, axis_index_groups=self.groups(self.feeders)).astype(F32)


def fence(*values):
    return lax.optimization_barrier(values)


def late(value, *others):
    return fence(value, *others)[0]


def chooser(sources, targets, source_of):
    row = lax.broadcasted_iota(jnp.int32, (sources, targets), 0)
    column = lax.broadcasted_iota(jnp.int32, (sources, targets), 1)
    return (row == source_of(column)).astype(BF16)


def shards(
    reps,
    places,
    tokens,
    segment_ids,
    norm_gain,
    input_weight,
    forget_weight,
    gate_weight,
    mixer_gain,
    out_weight,
    ffn_gain,
    ffn_gate_weight,
    ffn_up_weight,
    ffn_down_weight,
    cotangent,
):
    at = Place(reps, places)
    inputs = tokens[0].astype(F32)
    length, width = inputs.shape
    units = ffn_up_weight.shape[1]
    count = 2 ** len(at.mixers)
    channels = width // count
    part = units // 2 ** len(at.feeders)
    rows = width // places
    small = rows // reps
    slim = units // (places * reps)
    chip_rows = CORES * rows

    def channel_source(position):
        core, chip, inner = position // channels, position % channels // small, position % small
        return ((chip * CORES + core) * reps + at.r) * small + inner

    triple_rows = jnp.concatenate([input_weight, forget_weight, gate_weight])
    picked = matmul(triple_rows, chooser(width, CORES * channels, channel_source), (1, 0), BF16)
    picked = picked.reshape(3, rows, CORES, channels).transpose(1, 2, 0, 3).reshape(rows, -1)
    mix_all = lax.all_gather(picked, "shard", axis=0, tiled=True)

    pair_rows = jnp.concatenate([ffn_gate_weight, ffn_up_weight])

    def pick_units(core):
        def column(low):
            def source(position):
                line, inner = position // slim, position % slim
                return (((line * 2 + low) * CORES + core) * reps + at.r) * slim + inner

            return source

        return jnp.concatenate([matmul(pair_rows, chooser(units, part, column(low)), (1, 0), BF16) for low in range(2)])

    kept, given = pick_units(at.c), pick_units(1 - at.c)

    grad_out = cotangent[0]
    all_tokens = at.gather_members(tokens[0], at.mixers)
    segments = at.gather_members(segment_ids, at.mixers)
    starts = jnp.zeros((count, 1), F32)
    same = jnp.concatenate([starts, (segments[:, 1:] == segments[:, :-1]).astype(F32)], axis=1)
    same = same.reshape(count * length, 1)
    out_lines = at.join_his(at.own_rep(out_weight))
    out_lines, own_gains = fence(out_lines, jnp.stack([norm_gain, mixer_gain, ffn_gain]))
    out_lines = at.join(out_lines, at.lo, 1)
    out_other = at.swap(out_lines, at.low)
    gains = lax.all_gather(own_gains, "shard", axis=1, tiled=True).astype(F32)
    gain_one, gain_two, gain_three = gains[0], gains[1], gains[2]
    gain_grid = gain_two.reshape(at.chips, CORES, reps, small)
    gain_mix = lax.dynamic_index_in_dim(lax.dynamic_index_in_dim(gain_grid, at.c, 1, keepdims=False), at.r, 1, keepdims=False).reshape(-1)
    normed = (normalize(all_tokens.astype(F32))[0] * gain_one).astype(BF16)
    out_lines, normed = fence(out_lines, normed)
    out_rows = at.merge(out_lines, out_other, at.low, 2).reshape(channels, width)
    lines = lambda value: value.reshape(2 * CORES, rows, part)
    chip = at.merge(lines(kept), lines(at.swap(given, at.core)), at.core, 1).reshape(2, CORES * chip_rows, part)
    own_pair = at.trade(chip, at.low, 0)
    pair_grid = own_pair.reshape(2, 2, chip_rows, part)
    gate_half, up_half = pair_grid[:, 0].reshape(-1, part), pair_grid[:, 1].reshape(-1, part)
    mix_all, normed, same, gate_half, up_half, out_rows, grad_out_sent, own_down = fence(
        mix_all, normed, same, gate_half, up_half, out_rows, grad_out, at.own_rep(ffn_down_weight)
    )

    all_grad_out = at.gather_group(grad_out_sent)
    for which in at.his:
        gate_half = at.extend(gate_half, which)
    mix_weight = lax.dynamic_slice_in_dim(mix_all, at.c * (3 * channels), 3 * channels, 1)
    pre = matmul(normed, mix_weight, (1, 0))
    input_pre, forget_pre, gate_pre = (pre[:, k * channels : (k + 1) * channels] for k in range(3))
    forget = jax.nn.sigmoid(forget_pre)
    input_act, input_slope = swish_pair(input_pre)
    decay = forget * same
    state = run_scan(scan_forward_kernel, "scan_forward", count, length, decay, input_act * (1.0 - forget))
    gate_act, gate_slope = swish_pair(gate_pre)
    mixed_raw = (state * gain_mix * gate_act).astype(BF16)
    squares = jnp.sum(state * state, axis=1).reshape(count, length)
    out_part, squares, gate_half, up_half = fence(matmul(mixed_raw, out_rows, (1, 0), BF16), squares, gate_half, up_half)

    gate_columns = at.extend(gate_half, at.lo)
    for which in at.his:
        up_half = at.extend(up_half, which)
    square_sum = at.sum_members(squares, at.mixers)
    branch_sum = at.sum_members(out_part, at.mixers)
    branch_sum, square_sum, gate_columns, up_half, own_down = fence(branch_sum, square_sum, gate_columns, up_half, own_down)

    up_columns = at.extend(up_half, at.lo)
    down_lines = at.join_his(own_down)
    state_scale = lax.rsqrt(square_sum / width + EPSILON)
    branch = branch_sum * state_scale.reshape(length, 1)
    resid = inputs + branch
    scaled_mid, scale_mid = normalize(resid)
    ffn_in = at.gather_group(at.block_order((scaled_mid * gain_three).astype(BF16)))
    ffn_in, up_columns, down_lines, all_grad_out = fence(ffn_in, up_columns, down_lines, all_grad_out)
    down_rows = at.join(down_lines, at.lo, 1).reshape(part, width)
    ffn_gate = matmul(ffn_in, gate_columns, (1, 0))
    ffn_up = matmul(ffn_in, up_columns, (1, 0))
    ffn_act, ffn_slope = swish_pair(ffn_gate)
    hidden = (ffn_act * ffn_up).astype(BF16)
    down_cut = matmul(hidden, all_grad_out, (0, 0), BF16)
    down_rows, down_cut, hidden = fence(down_rows, down_cut, hidden)
    grad_hidden = matmul(all_grad_out, down_rows, (1, 1))
    grad_fgate = (grad_hidden * ffn_up * ffn_slope).astype(BF16)
    grad_fup = (grad_hidden * ffn_act).astype(BF16)
    grad_cut = (matmul(grad_fgate, gate_columns, (1, 1)) + matmul(grad_fup, up_columns, (1, 1))).astype(BF16)
    grad_cut, grad_fgate, grad_fup, down_cut = fence(grad_cut, grad_fgate, grad_fup, down_cut)

    grad_ffn_in = at.sum_group(grad_cut)
    down_line = at.reduce(down_cut.reshape(at.hi, 2, -1, width), at.lo, 1)
    gate_line = at.fold(matmul(ffn_in, grad_fgate, (0, 0), BF16), at.lo)
    up_cut = matmul(ffn_in, grad_fup, (0, 0), BF16)
    ffn_part = matmul(hidden, down_rows, (1, 0), BF16)
    down_line, ffn_part, up_cut = fence(down_line, ffn_part, up_cut)
    down_own = at.reduce_his(down_line)
    grad_ffn_in, gate_line, down_own, ffn_part, up_cut = fence(grad_ffn_in, gate_line, down_own, ffn_part, up_cut)

    def fold_begin(lines, which):
        half = lines.shape[0] // 2
        return (lines[:half], at.swap(lines[half:], which))

    def fold_rest(lines):
        for which in at.his[-2::-1]:
            lines = at.fold(lines, which)
        return lines

    mates = lambda lines: at.trade(lines.reshape(2, chip_rows, part), at.low, 0)
    cores = lambda sets: at.trade(sets.reshape(-1, CORES, rows, sets.shape[-1]), at.core, 1)
    up_line = at.fold(up_cut, at.lo)
    ffn_out = at.sum_group(ffn_part)
    grad_ffn_in = at.block_order(grad_ffn_in.astype(BF16), True).astype(F32)
    grad_resid = grad_out.astype(F32) + norm_back(grad_ffn_in * gain_three, scaled_mid, scale_mid)
    grad_branch_own = grad_resid.astype(BF16)
    inner_own = jnp.mean(grad_branch_own.astype(F32) * branch, axis=1)
    row_facts = at.gather_members(jnp.stack([state_scale.reshape(length), inner_own])[None], at.mixers)
    grad_branch = at.gather_members(grad_branch_own, at.mixers)
    grad_branch, row_facts, up_line, gate_line, down_own = fence(grad_branch, row_facts, up_line, gate_line, down_own)

    down_own = at.join_reps(down_own)
    gate_hi = fold_rest(at.end(*fold_begin(gate_line, at.his[-1])))
    all_scale = row_facts[:, 0].reshape(count * length, 1)
    all_inner = row_facts[:, 1].reshape(count * length, 1)
    state_scaled = state * all_scale
    mixed = (state_scaled * gain_mix * gate_act).astype(BF16)
    weighted = matmul(grad_branch, out_rows, (1, 1)) * gain_mix
    plane = lambda cut: cut.reshape(at.hi, 2, 2, -1, cut.shape[1])
    out_keep, out_other = at.begin(plane(matmul(mixed, grad_branch, (0, 0), BF16)), at.low, 2)
    grad_gate_pre = (weighted * state_scaled * gate_slope).astype(BF16)
    grad_state = all_scale * (weighted * gate_act - state_scaled * all_inner)
    carried = run_scan(scan_backward_kernel, "scan_backward", count, length, decay, grad_state)
    line = state.reshape(count, length, channels)
    previous = jnp.concatenate([jnp.zeros((count, 1, channels), F32), line[:, :-1]], axis=1).reshape(state.shape)
    grad_forget = carried * previous * same - carried * input_act
    grad_input_pre = (carried * (1.0 - forget) * input_slope).astype(BF16)
    grad_forget_pre = (grad_forget * forget * (1.0 - forget)).astype(BF16)
    cut_a, cut_b, cut_c = (plane(matmul(normed, g, (0, 0), BF16)) for g in (grad_gate_pre, grad_input_pre, grad_forget_pre))
    triple = jnp.concatenate([grad_input_pre, grad_forget_pre, grad_gate_pre], axis=1)
    normed_cut = matmul(triple, mix_weight, (1, 1), BF16)
    out_keep, cut_a, cut_b, cut_c, up_line, gate_hi, ffn_out, down_own, normed_cut = fence(
        out_keep, cut_a, cut_b, cut_c, up_line, gate_hi, ffn_out, down_own, normed_cut
    )

    def whole_units(own):
        grid = own.reshape(reps, CORES, 2, rows, at.length, slim)
        return grid.transpose(3, 4, 2, 1, 0, 5).reshape(rows, units).astype(F32)

    def whole_rows(own):
        return own.reshape(-1, width).astype(F32)

    sum_low = lambda cut: at.reduce(cut, at.low, 2)
    sum_lo = lambda line: at.reduce(line, at.lo, 1)
    gate_sets, out_low = mates(gate_hi), at.end(out_keep, out_other)
    keep_a, other_a = at.begin(cut_a, at.low, 2)
    gate_sets, out_low, keep_a, cut_b, cut_c, up_line, normed_cut, down_own = fence(
        gate_sets, out_low, keep_a, cut_b, cut_c, up_line, normed_cut, down_own
    )
    up_keep, up_other = fold_begin(up_line, at.his[-1])
    keep_b, other_b = at.begin(cut_b, at.low, 2)
    normed_half = at.sum_members(normed_cut, [at.core])
    low_a, out_lo, gate_cores = at.end(keep_a, other_a), sum_lo(out_low), cores(gate_sets)
    low_a, out_lo, gate_cores, up_keep, keep_b, cut_c, normed_half, down_own = fence(
        low_a, out_lo, gate_cores, up_keep, keep_b, cut_c, normed_half, down_own
    )
    up_hi = fold_rest(at.end(up_keep, up_other))
    grad_normed = at.sum_members(normed_half, at.rep_bits, BF16)
    up_sets = mates(up_hi)
    keep_c, other_c = at.begin(cut_c, at.low, 2)
    low_b, lo_a, out_own = at.end(keep_b, other_b), sum_lo(low_a), at.reduce_his(out_lo)
    low_b, lo_a, out_own, keep_c, up_sets, gate_cores = fence(low_b, lo_a, out_own, keep_c, up_sets, gate_cores)
    gate_own = at.join_reps(gate_cores)
    low_c, lo_b, hi_a, up_cores = at.end(keep_c, other_c), sum_lo(low_b), at.reduce_his(lo_a), cores(up_sets)
    low_c, lo_b, hi_a, up_cores, grad_normed = fence(low_c, lo_b, hi_a, up_cores, grad_normed)
    up_own, lo_c, hi_b, own_a = at.join_reps(up_cores), sum_lo(low_c), at.reduce_his(lo_b), cores(hi_a)
    lo_c, hi_b, own_a, out_own, gate_own, down_total = fence(lo_c, hi_b, own_a, out_own, gate_own, whole_rows(down_own))
    hi_c, own_b, own_a, out_own = at.reduce_his(lo_c), cores(hi_b), at.join_reps(own_a), at.join_reps(out_own)
    hi_c, own_b = fence(hi_c, own_b)
    own_c, own_b = cores(hi_c), at.join_reps(own_b)
    own_c, gate_own, up_own, out_own, grad_normed, ffn_out = fence(own_c, gate_own, up_own, out_own, grad_normed, ffn_out)
    mix_owns = [own_b, at.join_reps(own_c), own_a]
    block_output = (resid + ffn_out).astype(BF16)
    scaled_in, scale_in = normalize(inputs)
    input_grad = (grad_resid + norm_back(grad_normed * gain_one, scaled_in, scale_in)).astype(BF16)

    def channel_place(column):
        chip, core = column // (CORES * reps * small), column // (reps * small) % CORES
        return ((column // small % reps * CORES + core) * at.chips + chip) * small + column % small

    def whole_channels(owns):
        lines = jnp.stack(owns).reshape(len(owns), reps * CORES, rows, channels).transpose(0, 2, 1, 3).reshape(-1, width)
        return jnp.split(matmul(lines, chooser(width, width, channel_place), (1, 0)), len(owns))

    gate_total, up_total = whole_units(gate_own), whole_units(up_own)
    out_total = whole_rows(out_own)
    mix_totals = whole_channels(mix_owns)
    dotted = lambda w, g: jnp.sum(w.astype(F32) * g, axis=1)
    norm_gain_grad = sum(dotted(w, g) for w, g in zip((input_weight, forget_weight, gate_weight), mix_totals)) / norm_gain.astype(F32)
    mixer_gain_grad = dotted(out_weight, out_total) / mixer_gain.astype(F32)
    ffn_gain_grad = (dotted(ffn_gate_weight, gate_total) + dotted(ffn_up_weight, up_total)) / ffn_gain.astype(F32)
    return (
        block_output[None],
        input_grad[None],
        norm_gain_grad,
        *mix_totals,
        mixer_gain_grad,
        out_total,
        ffn_gain_grad,
        gate_total,
        up_total,
        down_total,
    )


def solution(mesh):
    tokens, vector, matrix = P(AXES, None, None), P("shard"), P("shard", None)
    placed = (tokens, P(AXES, None), vector, matrix, matrix, matrix, vector, matrix, vector, matrix, matrix, matrix, tokens)
    return jax.shard_map(
        functools.partial(shards, mesh.shape["rep"], mesh.shape["shard"]),
        mesh=mesh,
        in_specs=placed,
        out_specs=(tokens, tokens, vector, matrix, matrix, matrix, vector, matrix, vector, matrix, matrix, matrix),
        check_vma=False,
    )
```

```python
import functools

import jax
import jax.numpy as jnp
from jax import lax
from jax.experimental import pallas as pl
from jax.experimental.pallas import tpu as pltpu
from jax.sharding import PartitionSpec as P

EPSILON = 1e-06
AXES = ("rep", "shard")
CORES = 2
F32 = jnp.float32
BF16 = jnp.bfloat16


def normalize(values):
    scale = lax.rsqrt(jnp.mean(values * values, axis=-1, keepdims=True) + EPSILON)
    return (values * scale, scale)


def norm_back(grad_scaled, scaled, scale):
    inner = jnp.mean(grad_scaled * scaled, axis=-1, keepdims=True)
    return scale * (grad_scaled - scaled * inner)


def swish_pair(values):
    sigma = jax.nn.sigmoid(values)
    return (values * sigma, sigma * (1.0 + values * (1.0 - sigma)))


def matmul(left, right, dims, out=F32):
    return lax.dot_general(left, right, ((dims[:1], dims[1:]), ((), ())), preferred_element_type=F32).astype(out)


TILE = 8


def scan_tile(decay, update, reverse):
    row = lax.broadcasted_iota(jnp.int32, decay.shape, 0)
    for step in (1, 2, 4):
        shift = TILE - step if reverse else step
        inside = row < TILE - step if reverse else row >= step
        earlier = jnp.where(inside, pltpu.roll(update, shift, 0), 0.0)
        product = jnp.where(inside, pltpu.roll(decay, shift, 0), 1.0)
        update = update + decay * earlier
        decay = decay * product
    return (decay, update)


def scan_forward_kernel(count, length, decay, update, state):
    def block(step, carries):
        out = []
        for n in range(count):
            rows = pl.ds(pl.multiple_of(n * length + step * TILE, TILE), TILE)
            product, local = scan_tile(decay[rows, :], update[rows, :], False)
            local = local + product * carries[n]
            state[rows, :] = local
            out.append(local[TILE - 1 :, :])
        return tuple(out)

    lax.fori_loop(0, length // TILE, block, (jnp.zeros((1, state.shape[1]), F32),) * count)


def scan_backward_kernel(count, length, decay, grad, carried):
    steps = length // TILE

    def block(step, pairs):
        out = []
        for n in range(count):
            carry, later = pairs[n]
            rows = pl.ds(pl.multiple_of(n * length + (steps - 1 - step) * TILE, TILE), TILE)
            own = decay[rows, :]
            row = lax.broadcasted_iota(jnp.int32, own.shape, 0)
            following = jnp.where(row < TILE - 1, pltpu.roll(own, TILE - 1, 0), later)
            product, local = scan_tile(following, grad[rows, :], True)
            local = local + product * carry
            carried[rows, :] = local
            out.append((local[:1, :], own[:1, :]))
        return tuple(out)

    zero = jnp.zeros((1, carried.shape[1]), F32)
    lax.fori_loop(0, steps, block, ((zero, zero),) * count)


def run_scan(kernel, name, count, length, left, right):
    size = left.size
    return pl.pallas_call(
        functools.partial(kernel, count, length),
        out_shape=jax.ShapeDtypeStruct(left.shape, F32),
        in_specs=[pl.BlockSpec(memory_space=pltpu.VMEM)] * 2,
        out_specs=pl.BlockSpec(memory_space=pltpu.VMEM),
        compiler_params=pltpu.CompilerParams(vmem_limit_bytes=32 * 2**20),
        cost_estimate=pl.CostEstimate(flops=2 * size, bytes_accessed=12 * size, transcendentals=0),
        name=name,
    )(left, right)


def move_kernel(blocks, source, value, out):
    wide = value.shape[1] // blocks
    for k in range(blocks):
        out[:, k * wide : (k + 1) * wide] = value[:, pl.ds(pl.multiple_of(source[k] * wide, 128), wide)]


def move_blocks(source, value):
    return pl.pallas_call(
        functools.partial(move_kernel, source.shape[0]),
        out_shape=jax.ShapeDtypeStruct(value.shape, value.dtype),
        in_specs=[pl.BlockSpec(memory_space=pltpu.SMEM), pl.BlockSpec(memory_space=pltpu.VMEM)],
        out_specs=pl.BlockSpec(memory_space=pltpu.VMEM),
        cost_estimate=pl.CostEstimate(flops=0, bytes_accessed=2 * value.size * value.dtype.itemsize, transcendentals=0),
        name="move_blocks",
    )(source, value)


class Place:
    def __init__(self, reps, shards):
        self.reps, self.shards = reps, shards
        self.chips = shards // CORES
        self.hi = self.chips // 4
        self.length = self.chips // 2
        self.r = lax.axis_index("rep")
        self.s = lax.axis_index("shard")
        self.c = self.s % CORES
        self.core = ("shard", 1)
        self.low = ("shard", 2)
        self.lo = ("shard", 4)
        self.his = [("shard", 8 << k) for k in range(self.hi.bit_length() - 1)]
        self.rep_bits = [("rep", 1 << k) for k in range(reps.bit_length() - 1)]
        self.mixers = self.rep_bits + [self.core]
        self.feeders = self.rep_bits + [self.low, self.core]

    def bit(self, which):
        axis, value = which
        return ((self.r if axis == "rep" else self.s) // value) % 2

    def swap(self, value, which):
        axis, flip = which
        flip = flip * self.shards if axis == "rep" else flip
        return lax.ppermute(value, AXES, [(n, n ^ flip) for n in range(self.reps * self.shards)])

    def merge(self, own, other, which, axis=0):
        first = self.bit(which) == 0
        return jnp.stack([jnp.where(first, own, other), jnp.where(first, other, own)], axis)

    def join(self, value, which, axis=0):
        return self.merge(value, self.swap(value, which), which, axis)

    def pick(self, value, which, axis, flipped=False):
        bit = self.bit(which)
        return lax.dynamic_index_in_dim(value, 1 - bit if flipped else bit, axis, keepdims=False)

    def trade(self, value, which, axis):
        other = self.swap(self.pick(value, which, axis, True), which)
        return self.merge(self.pick(value, which, axis), other, which)

    def reduce(self, value, which, axis):
        other = self.swap(self.pick(value, which, axis, True), which)
        return (self.pick(value, which, axis).astype(F32) + other.astype(F32)).astype(BF16)

    def begin(self, value, which, axis):
        return (self.pick(value, which, axis), self.swap(self.pick(value, which, axis, True), which))

    def end(self, own, other):
        return (own.astype(F32) + other.astype(F32)).astype(BF16)

    def extend(self, value, which):
        return jnp.concatenate([value, self.swap(value, which)], axis=0)

    def fold(self, value, which):
        half = value.shape[0] // 2
        other = self.swap(value[half:], which)
        return (value[:half].astype(F32) + other.astype(F32)).astype(BF16)

    def block_order(self, value, back=False):
        place = jnp.arange(self.chips, dtype=jnp.int32)
        here = self.s // CORES & ~1
        if back:
            other = place ^ here
            return move_blocks(((other // 2 % 2) * self.hi + other // 4) * 2 + place % 2, value)
        hi, lo = place // 2 % self.hi, place // (2 * self.hi)
        return move_blocks((hi * 4 + lo * 2 + place % 2) ^ here, value)

    def gather_members(self, value, bits):
        for which in bits:
            value = jnp.concatenate([value, self.swap(value, which)], axis=0)
        return value

    def sum_members(self, partial, bits, wire=None):
        wire, total = wire or partial.dtype, partial
        for which in bits[::-1]:
            half = total.shape[0] // 2
            total = total[:half].astype(F32) + self.swap(total[half:].astype(wire), which).astype(F32)
        return total

    def join_his(self, value):
        for which in self.his:
            value = self.join(value, which)
        return value.reshape((self.hi,) + value.shape[len(self.his) :])

    def reduce_his(self, value):
        value = value.reshape((2,) * len(self.his) + value.shape[1:])
        for which in self.his[::-1]:
            value = self.reduce(value, which, 0)
        return value

    def join_reps(self, value):
        for which in self.rep_bits:
            value = self.join(value, which)
        return value.reshape((self.reps,) + value.shape[len(self.rep_bits) :])

    def own_rep(self, weight):
        return lax.dynamic_index_in_dim(weight.reshape(self.reps, -1, weight.shape[1]), self.r, 0, keepdims=False)

    def groups(self, bits):
        flips = [value * self.shards if axis == "rep" else value for axis, value in bits]
        group = [0]
        for flip in flips:
            group = group + [n + flip for n in group]
        group = sorted(group)
        return [[base + n for n in group] for base in range(self.reps * self.shards) if not base & sum(flips)]

    def gather_group(self, value):
        return lax.all_gather(value, AXES, axis=0, tiled=True, axis_index_groups=self.groups(self.feeders))

    def sum_group(self, value):
        return lax.psum_scatter(value, AXES, scatter_dimension=0, tiled=True, axis_index_groups=self.groups(self.feeders)).astype(F32)


def fence(*values):
    return lax.optimization_barrier(values)


def late(value, *others):
    return fence(value, *others)[0]


def chooser(sources, targets, source_of):
    row = lax.broadcasted_iota(jnp.int32, (sources, targets), 0)
    column = lax.broadcasted_iota(jnp.int32, (sources, targets), 1)
    return (row == source_of(column)).astype(BF16)


def shards(
    reps,
    places,
    tokens,
    segment_ids,
    norm_gain,
    input_weight,
    forget_weight,
    gate_weight,
    mixer_gain,
    out_weight,
    ffn_gain,
    ffn_gate_weight,
    ffn_up_weight,
    ffn_down_weight,
    cotangent,
):
    at = Place(reps, places)
    inputs = tokens[0].astype(F32)
    length, width = inputs.shape
    units = ffn_up_weight.shape[1]
    count = 2 ** len(at.mixers)
    channels = width // count
    part = units // 2 ** len(at.feeders)
    rows = width // places
    small = rows // reps
    slim = units // (places * reps)
    chip_rows = CORES * rows

    def channel_source(position):
        core, chip, inner = position // channels, position % channels // small, position % small
        return ((chip * CORES + core) * reps + at.r) * small + inner

    triple_rows = jnp.concatenate([input_weight, forget_weight, gate_weight])
    picked = matmul(triple_rows, chooser(width, CORES * channels, channel_source), (1, 0), BF16)
    picked = picked.reshape(3, rows, CORES, channels).transpose(1, 2, 0, 3).reshape(rows, -1)
    mix_all = lax.all_gather(picked, "shard", axis=0, tiled=True)

    pair_rows = jnp.concatenate([ffn_gate_weight, ffn_up_weight])

    def pick_units(core):
        def column(low):
            def source(position):
                line, inner = position // slim, position % slim
                return (((line * 2 + low) * CORES + core) * reps + at.r) * slim + inner

            return source

        return jnp.concatenate([matmul(pair_rows, chooser(units, part, column(low)), (1, 0), BF16) for low in range(2)])

    kept, given = pick_units(at.c), pick_units(1 - at.c)

    grad_out = cotangent[0]
    all_tokens = at.gather_members(tokens[0], at.mixers)
    segments = at.gather_members(segment_ids, at.mixers)
    starts = jnp.zeros((count, 1), F32)
    same = jnp.concatenate([starts, (segments[:, 1:] == segments[:, :-1]).astype(F32)], axis=1)
    same = same.reshape(count * length, 1)
    out_lines = at.join_his(at.own_rep(out_weight))
    out_lines, own_gains = fence(out_lines, jnp.stack([norm_gain, mixer_gain, ffn_gain]))
    out_lines = at.join(out_lines, at.lo, 1)
    out_other = at.swap(out_lines, at.low)
    gains = lax.all_gather(own_gains, "shard", axis=1, tiled=True).astype(F32)
    gain_one, gain_two, gain_three = gains[0], gains[1], gains[2]
    gain_grid = gain_two.reshape(at.chips, CORES, reps, small)
    gain_mix = lax.dynamic_index_in_dim(lax.dynamic_index_in_dim(gain_grid, at.c, 1, keepdims=False), at.r, 1, keepdims=False).reshape(-1)
    normed = (normalize(all_tokens.astype(F32))[0] * gain_one).astype(BF16)
    out_lines, normed = fence(out_lines, normed)
    out_rows = at.merge(out_lines, out_other, at.low, 2).reshape(channels, width)
    lines = lambda value: value.reshape(2 * CORES, rows, part)
    chip = at.merge(lines(kept), lines(at.swap(given, at.core)), at.core, 1).reshape(2, CORES * chip_rows, part)
    own_pair = at.trade(chip, at.low, 0)
    pair_grid = own_pair.reshape(2, 2, chip_rows, part)
    gate_half, up_half = pair_grid[:, 0].reshape(-1, part), pair_grid[:, 1].reshape(-1, part)
    mix_all, normed, same, gate_half, up_half, out_rows, grad_out_sent, own_down = fence(
        mix_all, normed, same, gate_half, up_half, out_rows, grad_out, at.own_rep(ffn_down_weight)
    )

    all_grad_out = at.gather_group(grad_out_sent)
    for which in at.his:
        gate_half = at.extend(gate_half, which)
    mix_weight = lax.dynamic_slice_in_dim(mix_all, at.c * (3 * channels), 3 * channels, 1)
    pre = matmul(normed, mix_weight, (1, 0))
    input_pre, forget_pre, gate_pre = (pre[:, k * channels : (k + 1) * channels] for k in range(3))
    forget = jax.nn.sigmoid(forget_pre)
    input_act, input_slope = swish_pair(input_pre)
    decay = forget * same
    state = run_scan(scan_forward_kernel, "scan_forward", count, length, decay, input_act * (1.0 - forget))
    gate_act, gate_slope = swish_pair(gate_pre)
    mixed_raw = (state * gain_mix * gate_act).astype(BF16)
    squares = jnp.sum(state * state, axis=1).reshape(count, length)
    out_part, squares, gate_half, up_half = fence(matmul(mixed_raw, out_rows, (1, 0), BF16), squares, gate_half, up_half)

    gate_columns = at.extend(gate_half, at.lo)
    for which in at.his:
        up_half = at.extend(up_half, which)
    square_sum = at.sum_members(squares, at.mixers)
    branch_sum = at.sum_members(out_part, at.mixers)
    branch_sum, square_sum, gate_columns, up_half, own_down = fence(branch_sum, square_sum, gate_columns, up_half, own_down)

    up_columns = at.extend(up_half, at.lo)
    down_lines = at.join_his(own_down)
    state_scale = lax.rsqrt(square_sum / width + EPSILON)
    branch = branch_sum * state_scale.reshape(length, 1)
    resid = inputs + branch
    scaled_mid, scale_mid = normalize(resid)
    ffn_in = at.gather_group(at.block_order((scaled_mid * gain_three).astype(BF16)))
    ffn_in, up_columns, down_lines, all_grad_out = fence(ffn_in, up_columns, down_lines, all_grad_out)
    down_rows = at.join(down_lines, at.lo, 1).reshape(part, width)
    ffn_gate = matmul(ffn_in, gate_columns, (1, 0))
    ffn_up = matmul(ffn_in, up_columns, (1, 0))
    ffn_act, ffn_slope = swish_pair(ffn_gate)
    hidden = (ffn_act * ffn_up).astype(BF16)
    down_cut = matmul(hidden, all_grad_out, (0, 0), BF16)
    down_rows, down_cut, hidden = fence(down_rows, down_cut, hidden)
    grad_hidden = matmul(all_grad_out, down_rows, (1, 1))
    grad_fgate = (grad_hidden * ffn_up * ffn_slope).astype(BF16)
    grad_fup = (grad_hidden * ffn_act).astype(BF16)
    grad_cut = (matmul(grad_fgate, gate_columns, (1, 1)) + matmul(grad_fup, up_columns, (1, 1))).astype(BF16)
    grad_cut, grad_fgate, grad_fup, down_cut = fence(grad_cut, grad_fgate, grad_fup, down_cut)

    grad_ffn_in = at.sum_group(grad_cut)
    down_line = at.reduce(down_cut.reshape(at.hi, 2, -1, width), at.lo, 1)
    gate_line = at.fold(matmul(ffn_in, grad_fgate, (0, 0), BF16), at.lo)
    up_cut = matmul(ffn_in, grad_fup, (0, 0), BF16)
    ffn_part = matmul(hidden, down_rows, (1, 0), BF16)
    down_line, ffn_part, up_cut = fence(down_line, ffn_part, up_cut)
    down_own = at.reduce_his(down_line)
    grad_ffn_in, gate_line, ffn_part, up_cut = fence(grad_ffn_in, gate_line, ffn_part, up_cut)

    def fold_begin(lines, which):
        half = lines.shape[0] // 2
        return (lines[:half], at.swap(lines[half:], which))

    def fold_rest(lines):
        for which in at.his[-2::-1]:
            lines = at.fold(lines, which)
        return lines

    mates = lambda lines: at.trade(lines.reshape(2, chip_rows, part), at.low, 0)
    cores = lambda sets: at.trade(sets.reshape(-1, CORES, rows, sets.shape[-1]), at.core, 1)
    up_line = at.fold(up_cut, at.lo)
    ffn_out = at.sum_group(ffn_part)
    grad_ffn_in = at.block_order(grad_ffn_in.astype(BF16), True).astype(F32)
    grad_resid = grad_out.astype(F32) + norm_back(grad_ffn_in * gain_three, scaled_mid, scale_mid)
    grad_branch_own = grad_resid.astype(BF16)
    inner_own = jnp.mean(grad_branch_own.astype(F32) * branch, axis=1)
    row_facts = at.gather_members(jnp.stack([state_scale.reshape(length), inner_own])[None], at.mixers)
    grad_branch = at.gather_members(grad_branch_own, at.mixers)
    grad_branch, row_facts, up_line, gate_line, down_own = fence(grad_branch, row_facts, up_line, gate_line, down_own)

    down_own = at.join_reps(down_own)
    gate_hi = fold_rest(at.end(*fold_begin(gate_line, at.his[-1])))
    all_scale = row_facts[:, 0].reshape(count * length, 1)
    all_inner = row_facts[:, 1].reshape(count * length, 1)
    state_scaled = state * all_scale
    mixed = (state_scaled * gain_mix * gate_act).astype(BF16)
    weighted = matmul(grad_branch, out_rows, (1, 1)) * gain_mix
    plane = lambda cut: cut.reshape(at.hi, 2, 2, -1, cut.shape[1])
    out_keep, out_other = at.begin(plane(matmul(mixed, grad_branch, (0, 0), BF16)), at.low, 2)
    grad_gate_pre = (weighted * state_scaled * gate_slope).astype(BF16)
    grad_state = all_scale * (weighted * gate_act - state_scaled * all_inner)
    carried = run_scan(scan_backward_kernel, "scan_backward", count, length, decay, grad_state)
    line = state.reshape(count, length, channels)
    previous = jnp.concatenate([jnp.zeros((count, 1, channels), F32), line[:, :-1]], axis=1).reshape(state.shape)
    grad_forget = carried * previous * same - carried * input_act
    grad_input_pre = (carried * (1.0 - forget) * input_slope).astype(BF16)
    grad_forget_pre = (grad_forget * forget * (1.0 - forget)).astype(BF16)
    cut_a, cut_b, cut_c = (plane(matmul(normed, g, (0, 0), BF16)) for g in (grad_gate_pre, grad_input_pre, grad_forget_pre))
    triple = jnp.concatenate([grad_input_pre, grad_forget_pre, grad_gate_pre], axis=1)
    normed_cut = matmul(triple, mix_weight, (1, 1), BF16)
    out_keep, cut_a, cut_b, cut_c, up_line, gate_hi, ffn_out, down_own, normed_cut = fence(
        out_keep, cut_a, cut_b, cut_c, up_line, gate_hi, ffn_out, down_own, normed_cut
    )

    def whole_units(own):
        grid = own.reshape(reps, CORES, 2, rows, at.length, slim)
        return grid.transpose(3, 4, 2, 1, 0, 5).reshape(rows, units).astype(F32)

    def whole_rows(own):
        return own.reshape(-1, width).astype(F32)

    sum_low = lambda cut: at.reduce(cut, at.low, 2)
    sum_lo = lambda line: at.reduce(line, at.lo, 1)
    gate_sets, out_low = mates(gate_hi), at.end(out_keep, out_other)
    keep_a, other_a = at.begin(cut_a, at.low, 2)
    gate_sets, out_low, keep_a, cut_b, cut_c, up_line, normed_cut, down_own = fence(
        gate_sets, out_low, keep_a, cut_b, cut_c, up_line, normed_cut, down_own
    )
    up_keep, up_other = fold_begin(up_line, at.his[-1])
    keep_b, other_b = at.begin(cut_b, at.low, 2)
    normed_half = at.sum_members(normed_cut, [at.core])
    low_a, out_lo, gate_cores = at.end(keep_a, other_a), sum_lo(out_low), cores(gate_sets)
    low_a, out_lo, gate_cores, up_keep, keep_b, cut_c, normed_half, down_own = fence(
        low_a, out_lo, gate_cores, up_keep, keep_b, cut_c, normed_half, down_own
    )
    up_hi = fold_rest(at.end(up_keep, up_other))
    grad_normed = at.sum_members(normed_half, at.rep_bits, BF16)
    up_sets = mates(up_hi)
    keep_c, other_c = at.begin(cut_c, at.low, 2)
    low_b, lo_a, out_own = at.end(keep_b, other_b), sum_lo(low_a), at.reduce_his(out_lo)
    low_b, lo_a, out_own, keep_c, up_sets, gate_cores = fence(low_b, lo_a, out_own, keep_c, up_sets, gate_cores)
    gate_own = at.join_reps(gate_cores)
    low_c, lo_b, hi_a, up_cores = at.end(keep_c, other_c), sum_lo(low_b), at.reduce_his(lo_a), cores(up_sets)
    low_c, lo_b, hi_a, up_cores, grad_normed = fence(low_c, lo_b, hi_a, up_cores, grad_normed)
    up_own, lo_c, hi_b, own_a = at.join_reps(up_cores), sum_lo(low_c), at.reduce_his(lo_b), cores(hi_a)
    lo_c, hi_b, own_a, out_own, gate_own, down_total = fence(lo_c, hi_b, own_a, out_own, gate_own, whole_rows(down_own))
    hi_c, own_b, own_a, out_own = at.reduce_his(lo_c), cores(hi_b), at.join_reps(own_a), at.join_reps(out_own)
    hi_c, own_b = fence(hi_c, own_b)
    own_c, own_b = cores(hi_c), at.join_reps(own_b)
    own_c, gate_own, up_own, out_own, grad_normed, ffn_out = fence(own_c, gate_own, up_own, out_own, grad_normed, ffn_out)
    mix_owns = [own_b, at.join_reps(own_c), own_a]
    block_output = (resid + ffn_out).astype(BF16)
    scaled_in, scale_in = normalize(inputs)
    input_grad = (grad_resid + norm_back(grad_normed * gain_one, scaled_in, scale_in)).astype(BF16)

    def channel_place(column):
        chip, core = column // (CORES * reps * small), column // (reps * small) % CORES
        return ((column // small % reps * CORES + core) * at.chips + chip) * small + column % small

    def whole_channels(owns):
        lines = jnp.stack(owns).reshape(len(owns), reps * CORES, rows, channels).transpose(0, 2, 1, 3).reshape(-1, width)
        return jnp.split(matmul(lines, chooser(width, width, channel_place), (1, 0)), len(owns))

    gate_total, up_total = whole_units(gate_own), whole_units(up_own)
    out_total = whole_rows(out_own)
    mix_totals = whole_channels(mix_owns)
    dotted = lambda w, g: jnp.sum(w.astype(F32) * g, axis=1)
    norm_gain_grad = sum(dotted(w, g) for w, g in zip((input_weight, forget_weight, gate_weight), mix_totals)) / norm_gain.astype(F32)
    mixer_gain_grad = dotted(out_weight, out_total) / mixer_gain.astype(F32)
    ffn_gain_grad = (dotted(ffn_gate_weight, gate_total) + dotted(ffn_up_weight, up_total)) / ffn_gain.astype(F32)
    return (
        block_output[None],
        input_grad[None],
        norm_gain_grad,
        *mix_totals,
        mixer_gain_grad,
        out_total,
        ffn_gain_grad,
        gate_total,
        up_total,
        down_total,
    )


def solution(mesh):
    tokens, vector, matrix = P(AXES, None, None), P("shard"), P("shard", None)
    placed = (tokens, P(AXES, None), vector, matrix, matrix, matrix, vector, matrix, vector, matrix, matrix, matrix, tokens)
    return jax.shard_map(
        functools.partial(shards, mesh.shape["rep"], mesh.shape["shard"]),
        mesh=mesh,
        in_specs=placed,
        out_specs=(tokens, tokens, vector, matrix, matrix, matrix, vector, matrix, vector, matrix, matrix, matrix),
        check_vma=False,
    )
```
